512 devices in a mesh: ctx: 256 (over y, x, z), kv: 2 (over core).
Axes of the slice: x: 4, y: 4, z: 16, core: 2. Of those that a mesh axis runs over, the one named last changes fastest.
Arguments:
- stretch_q: bfloat16 [32768, 5120], P('ctx', 'kv'), may hold values from -40 to 40
- stretch_do: bfloat16 [32768, 5120], P('ctx', 'kv'), may hold values from -24 to 24
- stretch_out: bfloat16 [32768, 5120], P('ctx', 'kv'), may hold values from -6 to 6
- stretch_lse: float32 [32768, 40], P('ctx', 'kv'), may hold values from -60 to 60, as said below
- stretch_pk: bfloat16 [128, 1024], P(None, 'kv'), may hold values from -20 to 20
- stretch_pv: bfloat16 [128, 1024], P(None, 'kv'), may hold values from -6 to 6
- global_q: bfloat16 [32768, 5120], P('ctx', 'kv'), may hold values from -40 to 40
- global_do: bfloat16 [32768, 5120], P('ctx', 'kv'), may hold values from -24 to 24
- global_out: bfloat16 [32768, 5120], P('ctx', 'kv'), may hold values from -6 to 6
- global_lse: float32 [32768, 40], P('ctx', 'kv'), may hold values from -60 to 60, as said below
- global_pk: bfloat16 [128, 1024], P(None, 'kv'), may hold values from -20 to 20
- global_pv: bfloat16 [128, 1024], P(None, 'kv'), may hold values from -6 to 6
- wq_stretch: bfloat16 [5120, 5120], P('ctx', 'kv'), may hold values from -0.5 to 0.5
- wk_stretch: bfloat16 [5120, 1024], P('ctx', 'kv'), may hold values from -0.5 to 0.5
- wv_stretch: bfloat16 [5120, 1024], P('ctx', 'kv'), may hold values from -0.5 to 0.5
- wq_global: bfloat16 [5120, 5120], P('ctx', 'kv'), may hold values from -0.5 to 0.5
- wk_global: bfloat16 [5120, 1024], P('ctx', 'kv'), may hold values from -0.5 to 0.5
- wv_global: bfloat16 [5120, 1024], P('ctx', 'kv'), may hold values from -0.5 to 0.5
Outputs:
- prompt_grad: float32 [128, 5120], P(None, 'ctx')
The draws below stay inside these ranges and needn't reach their ends.
Inputs may be any that keep to these rules, and one draw needn't show every extreme that they name: `stretch_lse`: saved log totals of the stretched layer: each at least the log of the sum of exp of its allowed prompt scores. `global_lse`: saved log totals of the global layer: each at least the log of the sum of exp of its allowed prompt scores.
All inputs are finite; a program needn't handle non-finite values.
Results may differ from the reference program's by a relative error of at most 0.0041.
Values may be sent and summed in bfloat16 or wider, within the bound.
A program may use at most 64 MiB of HBM per device.

```python
import math
import jax
import jax.numpy as jnp
from jax import lax

D = 5120
HD = 128
HPG = 5
KVG = 8
PROMPT = 128
SEQ = 32768
STRETCH = 8192


def layer_draw(key, salt, span):
    base_key = jax.random.fold_in(key, salt)
    subkeys = jax.random.split(base_key, 6)
    queries = jnp.clip(jax.random.normal(subkeys[0], (SEQ, KVG, HPG, HD), jnp.float32), -6.0, 6.0)
    key_rows = jnp.clip(jax.random.normal(subkeys[1], (PROMPT, KVG, HD), jnp.float32), -6.0, 6.0)
    common = jnp.clip(jax.random.normal(subkeys[2], (KVG, HD), jnp.float32), -4.0, 4.0)
    queries = queries + 0.5 * common[None, :, None, :]
    key_rows = key_rows + 0.55 * common[None, :, :]
    queries = queries.astype(jnp.bfloat16).astype(jnp.float32)
    key_rows = key_rows.astype(jnp.bfloat16).astype(jnp.float32)
    extra = jnp.exp(jax.random.uniform(subkeys[5], (SEQ, KVG, HPG), jnp.float32, math.log(0.5), math.log(4.0)))
    block_rows = math.gcd(SEQ, 512)
    ppos = jnp.arange(PROMPT)

    def block_lse(index):
        first_row = index * block_rows
        block_q = lax.dynamic_slice_in_dim(queries, first_row, block_rows, 0)
        scores = jnp.einsum('qghd,pgd->qghp', block_q, key_rows) * HD ** (-0.5)
        qpos = first_row + jnp.arange(block_rows)
        seen = (ppos[None, :] <= qpos[:, None])[:, None, None, :]
        inside = seen & (qpos < span)[:, None, None, None]
        top = jnp.max(jnp.where(seen, scores, -1e+30), -1)
        expd = jnp.where(seen, jnp.exp(scores - top[..., None]), 0.0)
        return (top, jnp.sum(jnp.where(inside, expd, 0.0), -1), jnp.sum(expd, -1))
    top, stretch_mass, all_mass = lax.map(block_lse, jnp.arange(SEQ // block_rows))
    top = top.reshape(SEQ, KVG, HPG)
    stretch_mass = stretch_mass.reshape(SEQ, KVG, HPG)
    all_mass = all_mass.reshape(SEQ, KVG, HPG)
    log_total = top + jnp.log(stretch_mass + extra * all_mass)
    return (queries.reshape(SEQ, KVG * HPG * HD), key_rows.reshape(PROMPT, KVG * HD), log_total.reshape(SEQ, KVG * HPG))


def draw_stretch_q(key, part):
    return layer_draw(key, 11, STRETCH)[0].astype(jnp.bfloat16)


def draw_stretch_pk(key, part):
    return layer_draw(key, 11, STRETCH)[1].astype(jnp.bfloat16)


def draw_stretch_lse(key, part):
    return layer_draw(key, 11, STRETCH)[2]


def draw_global_q(key, part):
    return layer_draw(key, 23, SEQ)[0].astype(jnp.bfloat16)


def draw_global_pk(key, part):
    return layer_draw(key, 23, SEQ)[1].astype(jnp.bfloat16)


def draw_global_lse(key, part):
    return layer_draw(key, 23, SEQ)[2]


def block_levels(rng, extent, cuts, low, largest):
    factor_of, own = 1.0, jax.random.fold_in(rng, 6)
    for dim, shards_of in cuts:
        heights = jnp.exp(jax.random.uniform(jax.random.fold_in(own, dim), (shards_of,), jnp.float32, low / len(cuts), largest / len(cuts)))
        factor_of = factor_of * jnp.repeat(heights, extent[dim] // shards_of).reshape([-1 if axis == dim else 1 for axis in range(len(extent))])
    return factor_of


def gaussian(rng, shape, spread, most, cuts=(), kind=jnp.bfloat16):
    values = jax.random.normal(rng, shape, jnp.float32) * spread
    if len(cuts) > 0:
        values = block_levels(rng, shape, cuts, -0.22, 0.18) * values
    return jnp.clip(values, min=-most, max=most).astype(kind)


def setup_inputs(seed: int = 0) -> dict:
    keys = jax.random.split(jax.random.key(seed), 19)
    return {
        "stretch_q": draw_stretch_q(jax.random.fold_in(keys[18], 71), 0),
        "stretch_do": gaussian(keys[1], (SEQ, KVG * HPG * HD), 4.0, 24.0, ((0, 256), (1, 2))),
        "stretch_out": gaussian(keys[2], (SEQ, KVG * HPG * HD), 1.0, 6.0, ((0, 256), (1, 2))),
        "stretch_lse": draw_stretch_lse(jax.random.fold_in(keys[18], 71), 0),
        "stretch_pk": draw_stretch_pk(jax.random.fold_in(keys[18], 71), 0),
        "stretch_pv": gaussian(keys[5], (PROMPT, KVG * HD), 1.0, 6.0, ((1, 2),)),
        "global_q": draw_global_q(jax.random.fold_in(keys[18], 71), 0),
        "global_do": gaussian(keys[7], (SEQ, KVG * HPG * HD), 4.0, 24.0, ((0, 256), (1, 2))),
        "global_out": gaussian(keys[8], (SEQ, KVG * HPG * HD), 1.0, 6.0, ((0, 256), (1, 2))),
        "global_lse": draw_global_lse(jax.random.fold_in(keys[18], 71), 0),
        "global_pk": draw_global_pk(jax.random.fold_in(keys[18], 71), 0),
        "global_pv": gaussian(keys[11], (PROMPT, KVG * HD), 1.0, 6.0, ((1, 2),)),
        "wq_stretch": gaussian(keys[12], (D, KVG * HPG * HD), HD ** -0.5, 0.5, ((0, 256), (1, 2))),
        "wk_stretch": gaussian(keys[13], (D, KVG * HD), HD ** -0.5, 0.5, ((0, 256), (1, 2))),
        "wv_stretch": gaussian(keys[14], (D, KVG * HD), HD ** -0.5, 0.5, ((0, 256), (1, 2))),
        "wq_global": gaussian(keys[15], (D, KVG * HPG * HD), HD ** -0.5, 0.5, ((0, 256), (1, 2))),
        "wk_global": gaussian(keys[16], (D, KVG * HD), HD ** -0.5, 0.5, ((0, 256), (1, 2))),
        "wv_global": gaussian(keys[17], (D, KVG * HD), HD ** -0.5, 0.5, ((0, 256), (1, 2))),
    }


def rounded(values):
    return lax.optimization_barrier(values.astype(jnp.bfloat16)).astype(jnp.float32)


def layer_grads(queries, cotangent, saved_out, log_total, prompt_k, prompt_v, span):
    inv_root = HD ** -0.5
    block_rows = math.gcd(SEQ, 512)
    block_count = SEQ // block_rows
    ppos = jnp.arange(PROMPT).astype(jnp.int32)
    grads_q, grads_k, grads_v = [], [], []
    for group_index in range(KVG):
        group_q = queries[:, group_index * HPG * HD:(group_index + 1) * HPG * HD].reshape(SEQ, HPG, HD)
        group_do = cotangent[:, group_index * HPG * HD:(group_index + 1) * HPG * HD].reshape(SEQ, HPG, HD)
        group_out = saved_out[:, group_index * HPG * HD:(group_index + 1) * HPG * HD].reshape(SEQ, HPG, HD)
        group_lse = log_total[:, group_index * HPG:(group_index + 1) * HPG]
        group_k = prompt_k[:, group_index * HD:(group_index + 1) * HD].astype(jnp.float32)
        group_v = prompt_v[:, group_index * HD:(group_index + 1) * HD].astype(jnp.float32)

        def block_terms(first_row, rows):
            block_q = lax.dynamic_slice_in_dim(group_q, first_row, rows, 0).astype(jnp.float32)
            block_do = lax.dynamic_slice_in_dim(group_do, first_row, rows, 0).astype(jnp.float32)
            block_out = lax.dynamic_slice_in_dim(group_out, first_row, rows, 0).astype(jnp.float32)
            block_lse = lax.dynamic_slice_in_dim(group_lse, first_row, rows, 0)
            scores = jnp.einsum('qhd,pd->hqp', block_q, group_k) * inv_root
            qpos = first_row + jnp.arange(rows).astype(jnp.int32)
            allowed = (ppos[None, :] <= qpos[:, None]) & (qpos[:, None] < span)
            probs = jnp.exp(jnp.where(allowed[None], scores - jnp.transpose(block_lse)[..., None], -jnp.inf))
            row_delta = jnp.transpose(jnp.sum(block_do * block_out, -1))
            grad_prob = jnp.einsum('qhd,pd->hqp', block_do, group_v)
            grad_score = rounded(probs * (grad_prob - row_delta[..., None]))
            return block_q, block_do, probs, grad_score

        def step(carry, block_index):
            acc_k, acc_v = carry
            first_row = (block_index * block_rows).astype(jnp.int32)
            block_q, block_do, probs, grad_score = block_terms(first_row, block_rows)
            acc_k = acc_k + jnp.einsum('hqp,qhd->pd', grad_score, block_q) * inv_root
            acc_v = acc_v + jnp.einsum('hqp,qhd->pd', rounded(probs), block_do)
            return (acc_k, acc_v), None

        zeros = jnp.zeros((PROMPT, HD), jnp.float32)
        (grad_k, grad_v), _ = lax.scan(step, (zeros, zeros), jnp.arange(block_count).astype(jnp.int32))
        _, _, _, head_score = block_terms(jnp.int32(0), PROMPT)
        grad_q = jnp.einsum('hqp,pd->qhd', head_score, group_k) * inv_root
        grads_q.append(grad_q.reshape(PROMPT, HPG * HD))
        grads_k.append(grad_k)
        grads_v.append(grad_v)
    return (jnp.concatenate(grads_q, 1).astype(jnp.bfloat16),
            jnp.concatenate(grads_k, 1).astype(jnp.bfloat16),
            jnp.concatenate(grads_v, 1).astype(jnp.bfloat16))


def reference(stretch_q, stretch_do, stretch_out, stretch_lse, stretch_pk, stretch_pv, global_q, global_do, global_out, global_lse, global_pk, global_pv, wq_stretch, wk_stretch, wv_stretch, wq_global, wk_global, wv_global):
    stretch_grads = layer_grads(stretch_q, stretch_do, stretch_out, stretch_lse, stretch_pk, stretch_pv, STRETCH)
    global_grads = layer_grads(global_q, global_do, global_out, global_lse, global_pk, global_pv, SEQ)
    result = jnp.zeros((PROMPT, D), jnp.float32)
    for grads, weights in ((stretch_grads, (wq_stretch, wk_stretch, wv_stretch)), (global_grads, (wq_global, wk_global, wv_global))):
        for grad_part, weight in zip(grads, weights):
            result = result + jnp.dot(grad_part, weight.T, preferred_element_type=jnp.float32)
    return result
```

```python
import functools

import jax
import jax.numpy as jnp
from jax import lax
from jax.experimental import pallas as pl
from jax.experimental.pallas import tpu as pltpu
from jax.sharding import PartitionSpec as P

HD = 128
HPG = 5
NEG = -1e30
PLANE = 16
MESH = pl.DeviceIdType.MESH
F32 = jnp.float32
BF16 = jnp.bfloat16


def nt(a, b):
    return lax.dot_general(a, b, (((1,), (1,)), ((), ())), preferred_element_type=F32)


def nn(a, b):
    return lax.dot_general(a, b, (((1,), (0,)), ((), ())), preferred_element_type=F32)


def unit_of(p):
    parity = (p % 4 + p // 4) % 2
    return p // 2 + 8 * (1 - parity)


def body(
    zs,
    sq, sdo, sout, slse, spk, spv,
    gq, gdo, gout, glse, gpk, gpv,
    wqs, wks, wvs, wqg, wkg, wvg,
    o_ref,
    q_buf, do_buf, out_buf, lse_buf, lse_t, pk_buf, pv_buf,
    w_kv, w_q, rw_kv, rw_q, wp,
    part, r_kv, s_buf, r_z,
    q_units, r_q, g_buf,
    o_send, r_o, half, r_half,
    load_sem, send_sem, recv_sem,
):
    me = lax.axis_index("ctx")
    kv = lax.axis_index("kv")
    pid = me // zs
    z = me % zs
    groups = pk_buf.shape[2] // HD
    tokens = q_buf.shape[1]
    width = groups * HPG * HD
    inv_root = HD ** (-0.5)
    near = pid < 4
    wide = pid < 8

    def plane_dev(p):
        return (p * zs + z, kv)

    def z_dev(zz):
        return (pid * zs + zz, kv)

    def send(src, dst, phase, dev):
        pltpu.make_async_remote_copy(
            src_ref=src, dst_ref=dst, send_sem=send_sem.at[phase], recv_sem=recv_sem.at[phase],
            device_id=dev, device_id_type=MESH,
        ).start()

    def wait_recv(ref, phase):
        pltpu.make_async_copy(ref, ref, recv_sem.at[phase]).wait()

    def wait_send(ref, phase):
        pltpu.make_async_copy(ref, ref, send_sem.at[phase]).wait()

    w_loads = []
    w_srcs = (
        (wks, w_kv, 0, 512), (wvs, w_kv, 512, 512), (wkg, w_kv, 1024, 512), (wvg, w_kv, 1536, 512),
        (wqs, w_q, 0, width), (wqg, w_q, width, width),
    )
    for n, (src, dst, start, size) in enumerate(w_srcs):
        w_loads.append(pltpu.make_async_copy(src, dst.at[:, pl.ds(start, size)], load_sem.at[n]))
    layer_loads = []
    for layer, srcs in enumerate(((sq, sdo, sout, slse, spk, spv), (gq, gdo, gout, glse, gpk, gpv))):
        dsts = (q_buf, do_buf, out_buf, lse_buf, pk_buf, pv_buf)
        layer_loads.append([
            pltpu.make_async_copy(s, d.at[layer], load_sem.at[6 + 6 * layer + n])
            for n, (s, d) in enumerate(zip(srcs, dsts))
        ])
    for c in w_loads:
        c.start()
    for c in layer_loads[1]:
        c.start()

    @pl.when(near)
    def _():
        for c in layer_loads[0]:
            c.start()

    barrier = pltpu.get_barrier_semaphore()

    @pl.loop(1, PLANE)
    def _(k):
        pl.semaphore_signal(barrier, inc=1, device_id=plane_dev((pid + k) % PLANE), device_id_type=MESH)

    @pl.loop(1, zs)
    def _(k):
        pl.semaphore_signal(barrier, inc=1, device_id=z_dev((z + k) % zs), device_id_type=MESH)

    pl.semaphore_signal(barrier, inc=1, device_id=(me, 1 - kv), device_id_type=MESH)

    wp[...] = jnp.zeros_like(wp)

    @pl.when(jnp.logical_not(wide))
    def _():
        g_buf[:, :, 384:512] = jnp.zeros((zs, 8, HD), BF16)

    for c in w_loads:
        c.wait()
    pl.semaphore_wait(barrier, (PLANE - 1) + (zs - 1) + 1)

    def q_start(p):
        return pl.multiple_of(jnp.where(p < 8, 384 * p, 3072 + 256 * (p - 8)), HD)

    @pl.loop(1, PLANE)
    def _(k):
        p = (pid + k) % PLANE
        u = unit_of(p)
        send(w_kv.at[:, pl.ds(pl.multiple_of(u * HD, HD), HD)], rw_kv.at[pid], 0, plane_dev(p))

        @pl.when(p < 8)
        def _():
            send(w_q.at[:, pl.ds(q_start(p), 384)], rw_q.at[pid], 1, plane_dev(p))

        @pl.when(p >= 8)
        def _():
            send(w_q.at[:, pl.ds(q_start(p), 256)], rw_q.at[pid, :, pl.ds(0, 256)], 1, plane_dev(p))

    def layer_terms(layer):
        for c in layer_loads[layer]:
            c.wait()
        pad = jnp.zeros((tokens, HD - groups * HPG), F32)
        lse_t[layer] = jnp.transpose(jnp.concatenate([lse_buf[layer], pad], axis=1))
        rows = lax.broadcasted_iota(jnp.int32, (HD, tokens), 0)
        cols = lax.broadcasted_iota(jnp.int32, (HD, tokens), 1) + me * tokens
        allowed = rows <= cols
        ones = jnp.ones((16, 2 * HD), BF16)
        for g in range(groups):
            heads = [pl.ds((g * HPG + h) * HD, HD) for h in range(HPG)]
            q_cat = jnp.concatenate([q_buf[layer, :, s] for s in heads], axis=0)
            do_cat = jnp.concatenate([do_buf[layer, :, s] for s in heads], axis=0)
            out_cat = jnp.concatenate([out_buf[layer, :, s] for s in heads], axis=0)
            key = pk_buf[layer, :, g * HD:(g + 1) * HD]
            val = pv_buf[layer, :, g * HD:(g + 1) * HD]
            prod = do_cat.astype(F32) * out_cat.astype(F32)
            high = prod.astype(BF16)
            low = (prod - high.astype(F32)).astype(BF16)
            delta = nt(ones, jnp.concatenate([high, low], axis=1))
            scores = nt(key, q_cat)
            grad_prob = nt(val, do_cat)
            p_parts, ds_parts = [], []
            for h in range(HPG):
                cut = slice(h * tokens, (h + 1) * tokens)
                row = g * HPG + h
                arg = scores[:, cut] * inv_root - lse_t[layer, row:row + 1, :]
                probs = jnp.exp(jnp.where(allowed, arg, NEG))
                p_parts.append(probs.astype(BF16))
                ds_parts.append((probs * (grad_prob[:, cut] - delta[0:1, cut])).astype(BF16))
            p_cat = jnp.concatenate(p_parts, axis=1)
            ds_cat = jnp.concatenate(ds_parts, axis=1)
            part[8 * layer + g] = (nn(ds_cat, q_cat) * inv_root).astype(BF16)
            part[8 * layer + 4 + g] = nn(p_cat, do_cat).astype(BF16)

            @pl.when(me == 0)
            def _():
                key_t = jnp.transpose(key.astype(F32)).astype(BF16)
                rows_t = nn(key_t, ds_cat) * inv_root
                q_units[:, pl.ds(layer * width + g * HPG * HD, HPG * HD)] = rows_t.astype(BF16)

    @pl.when(near)
    def _():
        layer_terms(0)

    layer_terms(1)

    @pl.when(me == 0)
    def _():
        @pl.loop(1, PLANE)
        def _(p):
            @pl.when(p < 8)
            def _():
                send(q_units.at[:, pl.ds(q_start(p), 384)], r_q, 2, plane_dev(p))

            @pl.when(p >= 8)
            def _():
                send(q_units.at[:, pl.ds(q_start(p), 256)], r_q.at[:, pl.ds(0, 256)], 2, plane_dev(p))

        r_q[...] = q_units[:, 0:384]

    my_unit = unit_of(pid)
    owns_global = my_unit >= 8

    @pl.loop(1, PLANE)
    def _(k):
        p = (pid + k) % PLANE
        u = unit_of(p)

        @pl.when(jnp.logical_or(near, u >= 8))
        def _():
            send(part.at[u], r_kv.at[pid], 3, plane_dev(p))

    @pl.when(jnp.logical_or(near, owns_global))
    def _():
        r_kv[pid] = part[my_unit]

    rw_kv[pid] = w_kv[:, pl.ds(pl.multiple_of(my_unit * HD, HD), HD)]

    @pl.when(wide)
    def _():
        rw_q[pid] = w_q[:, pl.ds(q_start(pid), 384)]
        wait_recv(rw_q.at[pl.ds(0, PLANE - 1)], 1)
        wp[:, 0:20, 128:512] = rw_q[...]

    @pl.when(jnp.logical_not(wide))
    def _():
        rw_q[pid, :, 0:256] = w_q[:, pl.ds(q_start(pid), 256)]
        wait_recv(rw_q.at[pl.ds(0, PLANE - 1), :, pl.ds(0, 256)], 1)
        wp[:, 0:20, 128:384] = rw_q[:, :, 0:256]

    wait_recv(rw_kv.at[pl.ds(0, PLANE - 1)], 0)
    wp[:, 0:20, 0:128] = rw_kv[...]

    @pl.when(owns_global)
    def _():
        wait_recv(r_kv.at[pl.ds(0, PLANE - 1)], 3)
        acc = r_kv[0].astype(F32)
        for n in range(1, PLANE):
            acc = acc + r_kv[n].astype(F32)
        s_buf[...] = acc

    @pl.when(jnp.logical_not(owns_global))
    def _():
        @pl.when(near)
        def _():
            wait_recv(r_kv.at[pl.ds(0, 3)], 3)

        @pl.when(jnp.logical_not(near))
        def _():
            wait_recv(r_kv.at[pl.ds(0, 4)], 3)

        acc = r_kv[0].astype(F32)
        for n in range(1, 4):
            acc = acc + r_kv[n].astype(F32)
        s_buf[...] = acc

    @pl.loop(1, zs)
    def _(k):
        zz = (z + k) % zs
        send(s_buf.at[pl.ds(pl.multiple_of(8 * zz, 8), 8)], r_z.at[z], 4, z_dev(zz))

    r_z[z] = s_buf[pl.ds(pl.multiple_of(8 * z, 8), 8), :]

    @pl.when(z == 0)
    def _():
        @pl.when(wide)
        def _():
            @pl.when(pid != 0)
            def _():
                wait_recv(r_q, 2)

            @pl.loop(1, zs)
            def _(zz):
                send(
                    r_q.at[pl.ds(pl.multiple_of(8 * zz, 8), 8)],
                    g_buf.at[zz, :, pl.ds(128, 384)], 5, z_dev(zz),
                )

            g_buf[0, :, 128:512] = r_q[0:8, :]

        @pl.when(jnp.logical_not(wide))
        def _():
            wait_recv(r_q.at[:, pl.ds(0, 256)], 2)

            @pl.loop(1, zs)
            def _(zz):
                send(
                    r_q.at[pl.ds(pl.multiple_of(8 * zz, 8), 8), pl.ds(0, 256)],
                    g_buf.at[zz, :, pl.ds(128, 256)], 5, z_dev(zz),
                )

            g_buf[0, :, 128:384] = r_q[0:8, 0:256]

    wait_recv(r_z.at[pl.ds(0, zs - 1)], 4)
    g_buf[z, :, 0:128] = jnp.sum(r_z[...], axis=0).astype(BF16)

    @pl.when(wide)
    def _():
        @pl.when(z != 0)
        def _():
            wait_recv(g_buf.at[0, :, pl.ds(128, 384)], 5)

        @pl.loop(1, zs)
        def _(k):
            send(g_buf.at[z], g_buf.at[z], 6, z_dev((z + k) % zs))

        wait_recv(g_buf.at[pl.ds(0, zs - 1)], 6)

    @pl.when(jnp.logical_not(wide))
    def _():
        @pl.when(z != 0)
        def _():
            wait_recv(g_buf.at[0, :, pl.ds(128, 256)], 5)

        @pl.loop(1, zs)
        def _(k):
            send(
                g_buf.at[z, :, pl.ds(0, 384)], g_buf.at[z, :, pl.ds(0, 384)], 6, z_dev((z + k) % zs)
            )

        wait_recv(g_buf.at[pl.ds(0, zs - 1), :, pl.ds(0, 384)], 6)

    g_kv = g_buf[:, :, 0:128].reshape(HD, HD)
    w_rows = wp[...].reshape(PLANE * 32, 512)
    total = nt(w_rows[:, 0:128], g_kv)
    for slot in range(3):
        cut = slice(128 * (slot + 1), 128 * (slot + 2))
        total = total + nn(w_rows[:, cut], g_buf[:, :, cut].reshape(HD, HD))
    o_send[...] = total.reshape(PLANE, 32, HD)

    @pl.loop(1, PLANE)
    def _(k):
        p = (pid + k) % PLANE
        send(o_send.at[p, pl.ds(0, 24)], r_o.at[pid], 7, plane_dev(p))

    r_o[pid] = o_send[pid, 0:24, :]
    wait_recv(r_o.at[pl.ds(0, PLANE - 1)], 7)
    half[...] = jnp.sum(r_o[...], axis=0)
    last = pltpu.make_async_remote_copy(
        src_ref=half, dst_ref=r_half, send_sem=send_sem.at[8], recv_sem=recv_sem.at[8],
        device_id=(me, 1 - kv), device_id_type=MESH,
    )
    last.start()

    wait_send(rw_kv.at[pl.ds(0, PLANE - 1)], 0)

    @pl.when(wide)
    def _():
        wait_send(rw_q.at[pl.ds(0, 7)], 1)
        wait_send(rw_q.at[pl.ds(0, 8), :, pl.ds(0, 256)], 1)
        wait_send(g_buf.at[pl.ds(0, zs - 1)], 6)

    @pl.when(jnp.logical_not(wide))
    def _():
        wait_send(rw_q.at[pl.ds(0, 8)], 1)
        wait_send(rw_q.at[pl.ds(0, 7), :, pl.ds(0, 256)], 1)
        wait_send(g_buf.at[pl.ds(0, zs - 1), :, pl.ds(0, 384)], 6)

    @pl.when(me == 0)
    def _():
        wait_send(q_units.at[:, pl.ds(0, 7 * 384 + 8 * 256)], 2)

    @pl.when(near)
    def _():
        wait_send(part.at[pl.ds(0, PLANE - 1)], 3)

    @pl.when(jnp.logical_and(jnp.logical_not(near), owns_global))
    def _():
        wait_send(part.at[pl.ds(0, 7)], 3)

    @pl.when(jnp.logical_and(jnp.logical_not(near), jnp.logical_not(owns_global)))
    def _():
        wait_send(part.at[pl.ds(0, 8)], 3)

    wait_send(r_z.at[pl.ds(0, zs - 1)], 4)

    @pl.when(jnp.logical_and(z == 0, wide))
    def _():
        wait_send(g_buf.at[pl.ds(0, zs - 1), :, pl.ds(128, 384)], 5)

    @pl.when(jnp.logical_and(z == 0, jnp.logical_not(wide)))
    def _():
        wait_send(g_buf.at[pl.ds(0, zs - 1), :, pl.ds(128, 256)], 5)

    wait_send(r_o.at[pl.ds(0, PLANE - 1)], 7)
    last.wait()
    both = half[...] + r_half[...]
    full = jnp.concatenate([both, jnp.zeros((HD - 24, HD), F32)], axis=0)
    o_ref[...] = jnp.transpose(full)[:, 0:20]


def solution(mesh):
    zs = mesh.shape["ctx"] // PLANE

    def local(*args):
        tokens, width = args[0].shape
        prompt, keys = args[4].shape
        cols = args[12].shape[0]
        heads = args[3].shape[1]
        any_spec = pl.BlockSpec(memory_space=pl.ANY)
        return pl.pallas_call(
            functools.partial(body, zs),
            out_shape=jax.ShapeDtypeStruct((prompt, cols), F32),
            in_specs=[any_spec] * 18,
            out_specs=pl.BlockSpec(memory_space=pltpu.VMEM),
            scratch_shapes=[
                pltpu.VMEM((2, tokens, width), BF16),
                pltpu.VMEM((2, tokens, width), BF16),
                pltpu.VMEM((2, tokens, width), BF16),
                pltpu.VMEM((2, tokens, heads), F32),
                pltpu.VMEM((2, HD, tokens), F32),
                pltpu.VMEM((2, prompt, keys), BF16),
                pltpu.VMEM((2, prompt, keys), BF16),
                pltpu.VMEM((cols, 4 * keys), BF16),
                pltpu.VMEM((cols, 2 * width), BF16),
                pltpu.VMEM((PLANE, cols, HD), BF16),
                pltpu.VMEM((PLANE, cols, 3 * HD), BF16),
                pltpu.VMEM((PLANE, 32, 4 * HD), BF16),
                pltpu.VMEM((PLANE, HD, HD), BF16),
                pltpu.VMEM((PLANE, HD, HD), BF16),
                pltpu.VMEM((HD, HD), F32),
                pltpu.VMEM((zs, 8, HD), F32),
                pltpu.VMEM((HD, 2 * width), BF16),
                pltpu.VMEM((HD, 3 * HD), BF16),
                pltpu.VMEM((zs, 8, 4 * HD), BF16),
                pltpu.VMEM((PLANE, 32, HD), F32),
                pltpu.VMEM((PLANE, 24, HD), F32),
                pltpu.VMEM((24, HD), F32),
                pltpu.VMEM((24, HD), F32),
                pltpu.SemaphoreType.DMA((18,)),
                pltpu.SemaphoreType.DMA((9,)),
                pltpu.SemaphoreType.DMA((9,)),
            ],
            compiler_params=pltpu.CompilerParams(
                collective_id=0, has_side_effects=True, vmem_limit_bytes=48 * 1024 * 1024
            ),
            name="prompt_grad",
        )(*args)

    split = P("ctx", "kv")
    keys = P(None, "kv")
    layer = (split, split, split, split, keys, keys)
    return jax.shard_map(
        local,
        mesh=mesh,
        in_specs=layer + layer + (split,) * 6,
        out_specs=P(None, "ctx"),
        check_vma=False,
    )
```

```python
import functools

import jax
import jax.numpy as jnp
from jax import lax
from jax.experimental import pallas as pl
from jax.experimental.pallas import tpu as pltpu
from jax.sharding import PartitionSpec as P

HD = 128
HPG = 5
NEG = -1e30
PLANE = 16
MESH = pl.DeviceIdType.MESH
F32 = jnp.float32
BF16 = jnp.bfloat16


def nt(a, b):
    return lax.dot_general(a, b, (((1,), (1,)), ((), ())), preferred_element_type=F32)


def nn(a, b):
    return lax.dot_general(a, b, (((1,), (0,)), ((), ())), preferred_element_type=F32)


def unit_of(p):
    parity = (p % 4 + p // 4) % 2
    return p // 2 + 8 * (1 - parity)


def pos_of(u):
    return next(p for p in range(PLANE) if unit_of(p) == u)


def pack(ds):
    strips = [ds[16 * s:16 * (s + 1)] for s in range(8)]
    rows = [strips[0]]
    for s in range(1, 4):
        rows.append(strips[s] + pltpu.roll(strips[8 - s], 16 * s, 1))
    rows.append(strips[4])
    return jnp.concatenate(rows, axis=0)


def unpack(packed):
    lane = lax.broadcasted_iota(jnp.int32, (16, HD), 1)
    rows = [packed[16 * s:16 * (s + 1)] for s in range(5)]
    low = [jnp.where(lane >= 16 * s, rows[s], 0.0) for s in range(1, 4)]
    high = [
        jnp.where(lane >= HD - 16 * s, pltpu.roll(rows[s], HD - 16 * s, 1), 0.0) for s in range(3, 0, -1)
    ]
    return jnp.concatenate([rows[0]] + low + [rows[4]] + high, axis=0)


W, SLOT, RS, ZRS, PASS, GATHER, OUT, CORE, FIRST = 0, 1, 4, 5, 6, 7, 8, 9, 10


def body(
    zs,
    sq, sdo, sout, slse, spk, spv,
    gq, gdo, gout, glse, gpk, gpv,
    wqs, wks, wvs, wqg, wkg, wvg,
    o_ref,
    q_buf, do_buf, out_buf, lse_buf, pk_buf, pv_buf,
    w_all, r_w, wp,
    part, r_kv, s_buf, r_z, g_buf,
    units, r_ds, key_t,
    o_send, r_o, half, r_half,
    load_sem, send_sem, recv_sem,
):
    me = lax.axis_index("ctx")
    kv = lax.axis_index("kv")
    pid = me // zs
    z = me % zs
    groups = pk_buf.shape[2] // HD
    heads = groups * HPG
    tokens = q_buf.shape[1]
    inv_root = HD ** (-0.5)
    near = pid < 4
    my_unit = unit_of(pid)
    owns_global = my_unit >= 8
    owns_near = my_unit < 8

    def plane_dev(p):
        return (p * zs + z, kv)

    def z_dev(zz):
        return (pid * zs + zz, kv)

    def send(src, dst, phase, dev, arrive=None):
        pltpu.make_async_remote_copy(
            src_ref=src, dst_ref=dst, send_sem=send_sem.at[phase],
            recv_sem=recv_sem.at[phase if arrive is None else arrive],
            device_id=dev, device_id_type=MESH,
        ).start()

    def wait_recv(ref, phase):
        pltpu.make_async_copy(ref, ref, recv_sem.at[phase]).wait()

    def wait_send(ref, phase):
        pltpu.make_async_copy(ref, ref, send_sem.at[phase]).wait()

    barrier = pltpu.get_barrier_semaphore()

    @pl.loop(0, zs - 1)
    def _(k):
        step = jnp.where(k % 2 == 0, zs // 2 + (k + 1) // 2, zs // 2 - (k + 1) // 2)
        pl.semaphore_signal(barrier, inc=1, device_id=z_dev((z + step) % zs), device_id_type=MESH)

    @pl.loop(1, PLANE)
    def _(k):
        pl.semaphore_signal(barrier, inc=1, device_id=plane_dev((pid + k) % PLANE), device_id_type=MESH)

    pl.semaphore_signal(barrier, inc=1, device_id=(me, 1 - kv), device_id_type=MESH)

    keys = groups * HD
    cut = 2048 - heads * HD
    layer_loads = []
    for layer, srcs in enumerate(((sq, sdo, sout, slse, spv, spk), (gq, gdo, gout, glse, gpv, gpk))):
        dsts = (q_buf, do_buf, out_buf, lse_buf, pv_buf, pk_buf)
        layer_loads.append([
            pltpu.make_async_copy(s, d.at[layer], load_sem.at[8 + 6 * layer + n])
            for n, (s, d) in enumerate(zip(srcs, dsts))
        ])
    w_srcs = (
        (wks, 0, 0, 0, keys), (wvs, 0, 0, keys, keys), (wkg, 0, 0, 2 * keys, keys), (wvg, 0, 0, 3 * keys, keys),
        (wqg, 0, 1, 0, 2048), (wqg, 2048, 2, 0, 512), (wqs, 0, 2, 512, 1536), (wqs, 1536, 3, 0, 1024),
    )
    w_loads = [
        pltpu.make_async_copy(
            src.at[:, pl.ds(first, size)], w_all.at[slot, :, pl.ds(start, size)], load_sem.at[n]
        )
        for n, (src, first, slot, start, size) in enumerate(w_srcs)
    ]
    for c in layer_loads[1]:
        c.start()
    layer_loads[0][5].start()

    @pl.when(near)
    def _():
        for c in layer_loads[0][:5]:
            c.start()

    for c in w_loads:
        c.start()

    wp[...] = jnp.zeros_like(wp)

    rows = lax.broadcasted_iota(jnp.int32, (HD, tokens), 0)
    cols = lax.broadcasted_iota(jnp.int32, (HD, tokens), 1) + me * tokens
    allowed = rows <= cols
    ones = jnp.ones((16, 2 * HD), BF16)

    def group_terms(layer, g):
        spans = [pl.ds((g * HPG + h) * HD, HD) for h in range(HPG)]
        q_cat = jnp.concatenate([q_buf[layer, :, s] for s in spans], axis=0)
        do_cat = jnp.concatenate([do_buf[layer, :, s] for s in spans], axis=0)
        out_cat = jnp.concatenate([out_buf[layer, :, s] for s in spans], axis=0)
        key = pk_buf[layer, :, g * HD:(g + 1) * HD]
        val = pv_buf[layer, :, g * HD:(g + 1) * HD]
        prod = do_cat.astype(F32) * out_cat.astype(F32)
        high = prod.astype(BF16)
        low = (prod - high.astype(F32)).astype(BF16)
        delta = nt(ones, jnp.concatenate([high, low], axis=1))
        scores = nt(key, q_cat)
        grad_prob = nt(val, do_cat)
        p_parts, ds_parts = [], []
        for h in range(HPG):
            span = slice(h * tokens, (h + 1) * tokens)
            row = g * HPG + h
            arg = scores[:, span] * inv_root - lse_buf[layer, row:row + 1, :]
            probs = jnp.exp(jnp.where(allowed, arg, NEG))
            p_parts.append(probs.astype(BF16))
            ds_parts.append((probs * (grad_prob[:, span] - delta[0:1, span])).astype(BF16))
        part[8 * layer + g] = (nn(jnp.concatenate(ds_parts, axis=1), q_cat) * inv_root).astype(BF16)
        part[8 * layer + 4 + g] = nn(jnp.concatenate(p_parts, axis=1), do_cat).astype(BF16)

        @pl.when(me == 0)
        def _():
            for h in range(HPG):
                units[(1 - layer) * heads + g * HPG + h] = pack(ds_parts[h].astype(F32)).astype(BF16)

    def send_units(first, last):
        for n in range(first, last):
            slot, p = n // 16, pos_of(n % 16)
            if p == 0:
                r_ds[slot] = units[n]
            else:
                send(units.at[n], r_ds.at[slot], FIRST, (p * zs, kv), SLOT + slot)

    for c in layer_loads[1]:
        c.wait()
    for g in range(groups):
        group_terms(1, g)

    pl.semaphore_wait(barrier, (PLANE - 1) + (zs - 1) + 1)

    @pl.when(me == 0)
    def _():
        send_units(0, heads)

    @pl.loop(1, PLANE)
    def _(k):
        p = (pid + k) % PLANE
        u = unit_of(p)

        @pl.when(u >= 8)
        def _():
            send(part.at[u], r_kv.at[pid], RS, plane_dev(p))

    layer_loads[0][5].wait()

    @pl.when(near)
    def _():
        for c in layer_loads[0][:5]:
            c.wait()
        for g in range(groups):
            group_terms(0, g)

            @pl.when(me == 0)
            def _():
                send_units(heads + g * HPG, heads + (g + 1) * HPG)

        @pl.loop(1, PLANE)
        def _(k):
            p = (pid + k) % PLANE
            u = unit_of(p)

            @pl.when(u < 8)
            def _():
                send(part.at[u], r_kv.at[pid], RS, plane_dev(p))

    @pl.when(jnp.logical_or(near, owns_global))
    def _():
        r_kv[pid] = part[my_unit]

    for c in w_loads:
        c.wait()

    @pl.when(owns_global)
    def _():
        wait_recv(r_kv.at[pl.ds(0, PLANE - 1)], RS)
        acc = r_kv[0].astype(F32)
        for n in range(1, PLANE):
            acc = acc + r_kv[n].astype(F32)
        s_buf[...] = acc

    @pl.when(owns_near)
    def _():
        @pl.when(near)
        def _():
            wait_recv(r_kv.at[pl.ds(0, 3)], RS)

        @pl.when(jnp.logical_not(near))
        def _():
            wait_recv(r_kv.at[pl.ds(0, 4)], RS)

        acc = r_kv[0].astype(F32)
        for n in range(1, 4):
            acc = acc + r_kv[n].astype(F32)
        s_buf[...] = acc

    @pl.loop(1, zs)
    def _(k):
        zz = (z + k) % zs
        send(s_buf.at[pl.ds(pl.multiple_of(8 * zz, 8), 8)], r_z.at[z], ZRS, z_dev(zz))

    r_z[z] = s_buf[pl.ds(pl.multiple_of(8 * z, 8), 8), :]

    def pass_on(slot):
        @pl.when(pid != 0)
        def _():
            wait_recv(r_ds.at[slot], SLOT + slot)

        @pl.loop(1, zs)
        def _(zz):
            send(r_ds.at[slot], r_ds.at[slot], PASS, z_dev(zz), SLOT + slot)

    @pl.when(z == 0)
    def _():
        pass_on(0)

    @pl.loop(1, PLANE)
    def _(k):
        p = (pid + k) % PLANE
        u = unit_of(p)
        lanes = pl.ds(pl.multiple_of(u * HD, HD), HD)

        @pl.when(u < 8)
        def _():
            send(w_all.at[:, :, lanes], r_w.at[pid], W, plane_dev(p))

        @pl.when(u >= 8)
        def _():
            send(w_all.at[pl.ds(0, 3), :, lanes], r_w.at[pid, pl.ds(0, 3)], W, plane_dev(p))

    @pl.when(z == 0)
    def _():
        pass_on(1)

        @pl.when(owns_near)
        def _():
            pass_on(2)

    def make_key(slot):
        n = 16 * slot + my_unit
        layer = jnp.where(n < heads, 1, 0)
        g = (n % heads) // HPG
        key = pk_buf[layer, :, pl.ds(pl.multiple_of(g * HD, HD), HD)]
        key_t[slot] = jnp.transpose(key.astype(F32)).astype(BF16)

    my_lanes = pl.ds(pl.multiple_of(my_unit * HD, HD), HD)
    for slot in range(3):
        r_w[pid, slot] = w_all[slot, :, my_lanes]
    make_key(0)
    make_key(1)

    @pl.when(owns_near)
    def _():
        r_w[pid, 3] = w_all[3, :, my_lanes]
        make_key(2)

    wait_recv(r_z.at[pl.ds(0, zs - 1)], ZRS)
    g_buf[z] = jnp.sum(r_z[...], axis=0).astype(BF16)

    @pl.loop(1, zs)
    def _(k):
        send(g_buf.at[z], g_buf.at[z], GATHER, z_dev((z + k) % zs))

    @pl.when(owns_near)
    def _():
        wait_recv(r_w.at[pl.ds(0, PLANE - 1)], W)
        wp[:, 0:20, 384:512] = r_w[:, 3]

    @pl.when(owns_global)
    def _():
        wait_recv(r_w.at[pl.ds(0, PLANE - 1), pl.ds(0, 3)], W)

    for slot in range(3):
        wp[:, 0:20, slot * HD:(slot + 1) * HD] = r_w[:, slot]

    def project(slot):
        ds = unpack(r_ds[slot].astype(F32)).astype(BF16)
        grad_q = (nn(key_t[slot], ds) * inv_root).astype(BF16)
        w_rows = wp[:, :, (slot + 1) * HD:(slot + 2) * HD].reshape(PLANE * 32, HD)
        return nn(w_rows, grad_q).reshape(PLANE, 32, HD)

    @pl.when(z != 0)
    def _():
        wait_recv(r_ds.at[0], SLOT)
        wait_recv(r_ds.at[1], SLOT + 1)

    o_send[...] = project(0) + project(1)

    @pl.when(owns_near)
    def _():
        @pl.when(z != 0)
        def _():
            wait_recv(r_ds.at[2], SLOT + 2)

        o_send[...] += project(2)

    wait_recv(g_buf.at[pl.ds(0, zs - 1)], GATHER)
    w_rows = wp[:, :, 0:HD].reshape(PLANE * 32, HD)
    o_send[...] += nt(w_rows, g_buf[...].reshape(HD, HD)).reshape(PLANE, 32, HD)

    @pl.loop(1, PLANE)
    def _(k):
        p = (pid + k) % PLANE
        send(o_send.at[p, pl.ds(0, 24)], r_o.at[pid], OUT, plane_dev(p))

    r_o[pid] = o_send[pid, 0:24, :]
    wait_recv(r_o.at[pl.ds(0, PLANE - 1)], OUT)
    half[...] = jnp.sum(r_o[...], axis=0)
    last = pltpu.make_async_remote_copy(
        src_ref=half, dst_ref=r_half, send_sem=send_sem.at[CORE], recv_sem=recv_sem.at[CORE],
        device_id=(me, 1 - kv), device_id_type=MESH,
    )
    last.start()

    @pl.when(me == 0)
    def _():
        wait_send(units.at[pl.ds(0, 2 * heads - 2)], FIRST)

    @pl.when(near)
    def _():
        wait_send(part.at[pl.ds(0, PLANE - 1)], RS)

    @pl.when(jnp.logical_and(jnp.logical_not(near), owns_global))
    def _():
        wait_send(part.at[pl.ds(0, 7)], RS)

    @pl.when(jnp.logical_and(jnp.logical_not(near), owns_near))
    def _():
        wait_send(part.at[pl.ds(0, 8)], RS)

    wait_send(r_z.at[pl.ds(0, zs - 1)], ZRS)

    @pl.when(z == 0)
    def _():
        for _ in range(2):
            wait_send(units.at[pl.ds(0, zs - 1)], PASS)

        @pl.when(owns_near)
        def _():
            wait_send(units.at[pl.ds(0, zs - 1)], PASS)

    @pl.when(owns_near)
    def _():
        wait_send(r_w.at[pl.ds(0, 7)], W)
        wait_send(r_w.at[pl.ds(0, 8), pl.ds(0, 3)], W)

    @pl.when(owns_global)
    def _():
        wait_send(r_w.at[pl.ds(0, 8)], W)
        wait_send(r_w.at[pl.ds(0, 7), pl.ds(0, 3)], W)

    wait_send(g_buf.at[pl.ds(0, zs - 1)], GATHER)
    wait_send(r_o.at[pl.ds(0, PLANE - 1)], OUT)
    last.wait()
    o_ref[...] = (half[...] + r_half[...])[0:20, :]


def solution(mesh):
    zs = mesh.shape["ctx"] // PLANE

    def local(*args):
        tokens, width = args[0].shape
        prompt, keys = args[4].shape
        cols = args[12].shape[0]
        heads = args[3].shape[1]
        any_spec = pl.BlockSpec(memory_space=pltpu.HBM)
        args = [jnp.transpose(a) if n in (3, 9) else a for n, a in enumerate(args)]
        out = pl.pallas_call(
            functools.partial(body, zs),
            out_shape=jax.ShapeDtypeStruct((cols, prompt), F32),
            in_specs=[any_spec] * 18,
            out_specs=pl.BlockSpec(memory_space=pltpu.VMEM),
            scratch_shapes=[
                pltpu.VMEM((2, tokens, width), BF16),
                pltpu.VMEM((2, tokens, width), BF16),
                pltpu.VMEM((2, tokens, width), BF16),
                pltpu.VMEM((2, heads, tokens), F32),
                pltpu.VMEM((2, prompt, keys), BF16),
                pltpu.VMEM((2, prompt, keys), BF16),
                pltpu.VMEM((4, cols, PLANE * HD), BF16),
                pltpu.VMEM((PLANE, 4, cols, HD), BF16),
                pltpu.VMEM((PLANE, 32, 4 * HD), BF16),
                pltpu.VMEM((PLANE, HD, HD), BF16),
                pltpu.VMEM((PLANE, HD, HD), BF16),
                pltpu.VMEM((HD, HD), F32),
                pltpu.VMEM((zs, 8, HD), F32),
                pltpu.VMEM((zs, 8, HD), BF16),
                pltpu.VMEM((2 * heads, 80, HD), BF16),
                pltpu.VMEM((3, 80, HD), BF16),
                pltpu.VMEM((3, HD, HD), BF16),
                pltpu.VMEM((PLANE, 32, HD), F32),
                pltpu.VMEM((PLANE, 24, HD), F32),
                pltpu.VMEM((24, HD), F32),
                pltpu.VMEM((24, HD), F32),
                pltpu.SemaphoreType.DMA((20,)),
                pltpu.SemaphoreType.DMA((11,)),
                pltpu.SemaphoreType.DMA((11,)),
            ],
            compiler_params=pltpu.CompilerParams(
                collective_id=0, has_side_effects=True, vmem_limit_bytes=60 * 1024 * 1024
            ),
            name="prompt_grad",
        )(*args)
        return jnp.transpose(out)

    split = P("ctx", "kv")
    keys = P(None, "kv")
    layer = (split, split, split, split, keys, keys)
    return jax.shard_map(
        local,
        mesh=mesh,
        in_specs=layer + layer + (split,) * 6,
        out_specs=P(None, "ctx"),
        check_vma=False,
    )
```

```python
import functools

import jax
import jax.numpy as jnp
from jax import lax
from jax.experimental import pallas as pl
from jax.experimental.pallas import tpu as pltpu
from jax.sharding import PartitionSpec as P

HD = 128
HPG = 5
NEG = -1e30
PLANE = 16
MESH = pl.DeviceIdType.MESH
F32 = jnp.float32
BF16 = jnp.bfloat16


def nt(a, b):
    return lax.dot_general(a, b, (((1,), (1,)), ((), ())), preferred_element_type=F32)


def nn(a, b):
    return lax.dot_general(a, b, (((1,), (0,)), ((), ())), preferred_element_type=F32)


def unit_of(p):
    parity = (p % 4 + p // 4) % 2
    return p // 2 + 8 * (1 - parity)


OFFSETS = (
    (2, 2), (2, 1), (1, 2), (2, 3), (3, 2), (1, 1), (3, 3), (1, 3), (3, 1), (2, 0), (0, 2), (1, 0), (0, 1),
    (3, 0), (0, 3),
)


HEADS = ((0,) * 16, ((4,) * 4 + (12,) * 4) * 2, (12,) * 4 + (4,) * 4)


def pos_of(u):
    return next(p for p in range(PLANE) if unit_of(p) == u)


def pack(ds):
    strips = [ds[16 * s:16 * (s + 1)] for s in range(8)]
    rows = [strips[0]]
    for s in range(1, 4):
        rows.append(strips[s] + pltpu.roll(strips[8 - s], 16 * s, 1))
    rows.append(strips[4])
    return jnp.concatenate(rows, axis=0)


def unpack(packed):
    lane = lax.broadcasted_iota(jnp.int32, (16, HD), 1)
    rows = [packed[16 * s:16 * (s + 1)] for s in range(5)]
    low = [jnp.where(lane >= 16 * s, rows[s], 0.0) for s in range(1, 4)]
    high = [
        jnp.where(lane >= HD - 16 * s, pltpu.roll(rows[s], HD - 16 * s, 1), 0.0) for s in range(3, 0, -1)
    ]
    return jnp.concatenate([rows[0]] + low + [rows[4]] + high, axis=0)


W, SLOT, RS, ZRS, PASS, GATHER, OUT, CORE, FIRST = 0, 1, 4, 5, 6, 7, 8, 9, 10


def body(
    zs,
    sq, sdo, sout, slse, spk, spv,
    gq, gdo, gout, glse, gpk, gpv,
    wqs, wks, wvs, wqg, wkg, wvg,
    o_ref,
    q_buf, do_buf, out_buf, lse_buf, pk_buf, pv_buf,
    w_all, r_w, wp,
    part, r_kv, s_buf, r_z, g_buf,
    units, r_ds, key_t,
    o_send, r_o, half, r_half,
    load_sem, send_sem, recv_sem,
):
    me = lax.axis_index("ctx")
    kv = lax.axis_index("kv")
    pid = me // zs
    z = me % zs
    groups = pk_buf.shape[2] // HD
    heads = groups * HPG
    tokens = q_buf.shape[1]
    inv_root = HD ** (-0.5)
    near = pid < 4
    my_unit = unit_of(pid)
    owns_global = my_unit >= 8
    owns_near = my_unit < 8

    row, col = pid // 4, pid % 4

    def peers():
        for dy, dx in OFFSETS:
            yield ((row + dy) % 4) * 4 + (col + dx) % 4

    def far(k):
        step = jnp.where(k % 2 == 0, zs // 2 + (k + 1) // 2, zs // 2 - (k + 1) // 2)
        return (z + step) % zs

    def plane_dev(p):
        return (p * zs + z, kv)

    def z_dev(zz):
        return (pid * zs + zz, kv)

    def send(src, dst, phase, dev, arrive=None):
        pltpu.make_async_remote_copy(
            src_ref=src, dst_ref=dst, send_sem=send_sem.at[phase],
            recv_sem=recv_sem.at[phase if arrive is None else arrive],
            device_id=dev, device_id_type=MESH,
        ).start()

    def wait_recv(ref, phase):
        pltpu.make_async_copy(ref, ref, recv_sem.at[phase]).wait()

    def wait_send(ref, phase):
        pltpu.make_async_copy(ref, ref, send_sem.at[phase]).wait()

    heads_z = (0, jnp.where(my_unit // 4 % 2 == 0, 4, 12), jnp.where(my_unit < 4, 12, 4))
    heads_me = (
        z == 0, z == heads_z[1], jnp.logical_and(owns_near, z == heads_z[2]),
    )

    barrier = pltpu.get_barrier_semaphore()

    @pl.loop(0, zs - 1)
    def _(k):
        pl.semaphore_signal(barrier, inc=1, device_id=z_dev(far(k)), device_id_type=MESH)

    for p in peers():
        pl.semaphore_signal(barrier, inc=1, device_id=plane_dev(p), device_id_type=MESH)

    pl.semaphore_signal(barrier, inc=1, device_id=(me, 1 - kv), device_id_type=MESH)

    for slot in (1, 2):
        @pl.when(jnp.logical_and(pid != 0, heads_me[slot]))
        def _():
            pl.semaphore_signal(barrier, inc=1, device_id=(0, kv), device_id_type=MESH)

    keys = groups * HD
    cut = 2048 - heads * HD
    layer_loads = []
    for layer, srcs in enumerate(((sq, sdo, sout, slse, spv, spk), (gq, gdo, gout, glse, gpv, gpk))):
        dsts = (q_buf, do_buf, out_buf, lse_buf, pv_buf, pk_buf)
        layer_loads.append([
            pltpu.make_async_copy(s, d.at[layer], load_sem.at[8 + 6 * layer + n])
            for n, (s, d) in enumerate(zip(srcs, dsts))
        ])
    w_srcs = (
        (wks, 0, 0, 0, keys), (wvs, 0, 0, keys, keys), (wkg, 0, 0, 2 * keys, keys), (wvg, 0, 0, 3 * keys, keys),
        (wqg, 0, 1, 0, 2048), (wqg, 2048, 2, 0, 512), (wqs, 0, 2, 512, 1536), (wqs, 1536, 3, 0, 1024),
    )
    w_loads = [
        pltpu.make_async_copy(
            src.at[:, pl.ds(first, size)], w_all.at[slot, :, pl.ds(start, size)], load_sem.at[n]
        )
        for n, (src, first, slot, start, size) in enumerate(w_srcs)
    ]
    for c in layer_loads[1]:
        c.start()
    layer_loads[0][5].start()

    @pl.when(near)
    def _():
        for c in layer_loads[0][:5]:
            c.start()

    for c in w_loads:
        c.start()

    wp[...] = jnp.zeros_like(wp)

    rows = lax.broadcasted_iota(jnp.int32, (HD, tokens), 0)
    cols = lax.broadcasted_iota(jnp.int32, (HD, tokens), 1) + me * tokens
    allowed = rows <= cols
    ones = jnp.ones((16, 2 * HD), BF16)

    def group_terms(layer, g):
        spans = [pl.ds((g * HPG + h) * HD, HD) for h in range(HPG)]
        q_cat = jnp.concatenate([q_buf[layer, :, s] for s in spans], axis=0)
        do_cat = jnp.concatenate([do_buf[layer, :, s] for s in spans], axis=0)
        out_cat = jnp.concatenate([out_buf[layer, :, s] for s in spans], axis=0)
        key = pk_buf[layer, :, g * HD:(g + 1) * HD]
        val = pv_buf[layer, :, g * HD:(g + 1) * HD]
        prod = do_cat.astype(F32) * out_cat.astype(F32)
        high = prod.astype(BF16)
        low = (prod - high.astype(F32)).astype(BF16)
        delta = nt(ones, jnp.concatenate([high, low], axis=1))
        scores = nt(key, q_cat)
        grad_prob = nt(val, do_cat)
        p_parts, ds_parts = [], []
        for h in range(HPG):
            span = slice(h * tokens, (h + 1) * tokens)
            row = g * HPG + h
            arg = scores[:, span] * inv_root - lse_buf[layer, row:row + 1, :]
            probs = jnp.exp(jnp.where(allowed, arg, NEG))
            p_parts.append(probs.astype(BF16))
            ds_parts.append((probs * (grad_prob[:, span] - delta[0:1, span])).astype(BF16))
        part[8 * layer + g] = (nn(jnp.concatenate(ds_parts, axis=1), q_cat) * inv_root).astype(BF16)
        part[8 * layer + 4 + g] = nn(jnp.concatenate(p_parts, axis=1), do_cat).astype(BF16)

        @pl.when(me == 0)
        def _():
            for h in range(HPG):
                units[(1 - layer) * heads + g * HPG + h] = pack(ds_parts[h].astype(F32)).astype(BF16)

    def send_units():
        for u in range(PLANE):
            p = pos_of(u)
            for slot in range(3 if u < 8 else 2):
                n = 16 * slot + u
                head = HEADS[slot][u]
                if p == 0 and head == 0:
                    r_ds[slot] = units[n]
                else:
                    send(units.at[n], r_ds.at[slot], FIRST, (p * zs + head, kv), SLOT + slot)

    for c in layer_loads[1]:
        c.wait()
    for g in range(groups):
        group_terms(1, g)
    layer_loads[0][5].wait()

    @pl.when(near)
    def _():
        for c in layer_loads[0][:5]:
            c.wait()
        for g in range(groups):
            group_terms(0, g)

    greeted = (PLANE - 1) + (zs - 1) + 1
    pl.semaphore_wait(barrier, jnp.where(me == 0, greeted + 23, greeted))

    for p in peers():
        u = unit_of(p)

        @pl.when(jnp.logical_or(near, u >= 8))
        def _():
            send(part.at[u], r_kv.at[pid], RS, plane_dev(p))

    @pl.when(me == 0)
    def _():
        send_units()

    @pl.when(jnp.logical_or(near, owns_global))
    def _():
        r_kv[pid] = part[my_unit]

    for c in w_loads:
        c.wait()

    @pl.when(owns_global)
    def _():
        wait_recv(r_kv.at[pl.ds(0, PLANE - 1)], RS)
        acc = r_kv[0].astype(F32)
        for n in range(1, PLANE):
            acc = acc + r_kv[n].astype(F32)
        s_buf[...] = acc

    @pl.when(owns_near)
    def _():
        @pl.when(near)
        def _():
            wait_recv(r_kv.at[pl.ds(0, 3)], RS)

        @pl.when(jnp.logical_not(near))
        def _():
            wait_recv(r_kv.at[pl.ds(0, 4)], RS)

        acc = r_kv[0].astype(F32)
        for n in range(1, 4):
            acc = acc + r_kv[n].astype(F32)
        s_buf[...] = acc

    @pl.loop(0, zs - 1)
    def _(k):
        zz = far(k)
        send(s_buf.at[pl.ds(pl.multiple_of(8 * zz, 8), 8)], r_z.at[z], ZRS, z_dev(zz))

    r_z[z] = s_buf[pl.ds(pl.multiple_of(8 * z, 8), 8), :]

    def pass_on(slot):
        @pl.when(pid != 0 if slot == 0 else me >= 0)
        def _():
            wait_recv(r_ds.at[slot], SLOT + slot)

        @pl.loop(0, zs - 1)
        def _(k):
            send(r_ds.at[slot], r_ds.at[slot], PASS, z_dev(far(k)), SLOT + slot)

    for p in peers():
        u = unit_of(p)
        lanes = pl.ds(pl.multiple_of(u * HD, HD), HD)

        @pl.when(u < 8)
        def _():
            send(w_all.at[:, :, lanes], r_w.at[pid], W, plane_dev(p))

        @pl.when(u >= 8)
        def _():
            send(w_all.at[pl.ds(0, 3), :, lanes], r_w.at[pid, pl.ds(0, 3)], W, plane_dev(p))

    @pl.when(heads_me[0])
    def _():
        pass_on(0)

    def make_key(slot):
        n = 16 * slot + my_unit
        layer = jnp.where(n < heads, 1, 0)
        g = (n % heads) // HPG
        key = pk_buf[layer, :, pl.ds(pl.multiple_of(g * HD, HD), HD)]
        key_t[slot] = jnp.transpose(key.astype(F32)).astype(BF16)

    my_lanes = pl.ds(pl.multiple_of(my_unit * HD, HD), HD)
    for slot in range(3):
        r_w[pid, slot] = w_all[slot, :, my_lanes]
    make_key(0)
    make_key(1)

    @pl.when(owns_near)
    def _():
        r_w[pid, 3] = w_all[3, :, my_lanes]
        make_key(2)

    wait_recv(r_z.at[pl.ds(0, zs - 1)], ZRS)
    g_buf[z] = jnp.sum(r_z[...], axis=0).astype(BF16)

    @pl.loop(0, zs - 1)
    def _(k):
        send(g_buf.at[z], g_buf.at[z], GATHER, z_dev(far(k)))

    @pl.when(heads_me[1])
    def _():
        pass_on(1)

    @pl.when(heads_me[2])
    def _():
        pass_on(2)

    @pl.when(owns_near)
    def _():
        wait_recv(r_w.at[pl.ds(0, PLANE - 1)], W)
        wp[:, 0:20, 384:512] = r_w[:, 3]

    @pl.when(owns_global)
    def _():
        wait_recv(r_w.at[pl.ds(0, PLANE - 1), pl.ds(0, 3)], W)

    for slot in range(3):
        wp[:, 0:20, slot * HD:(slot + 1) * HD] = r_w[:, slot]

    def project(slot):
        ds = unpack(r_ds[slot].astype(F32)).astype(BF16)
        grad_q = (nn(key_t[slot], ds) * inv_root).astype(BF16)
        w_rows = wp[:, :, (slot + 1) * HD:(slot + 2) * HD].reshape(PLANE * 32, HD)
        return nn(w_rows, grad_q).reshape(PLANE, 32, HD)[:, 0:20]

    for slot in range(2):
        @pl.when(z != heads_z[slot])
        def _():
            wait_recv(r_ds.at[slot], SLOT + slot)

    o_send[...] = project(0) + project(1)

    @pl.when(owns_near)
    def _():
        @pl.when(z != heads_z[2])
        def _():
            wait_recv(r_ds.at[2], SLOT + 2)

        o_send[...] += project(2)

    wait_recv(g_buf.at[pl.ds(0, zs - 1)], GATHER)
    w_rows = wp[:, :, 0:HD].reshape(PLANE * 32, HD)
    o_send[...] += nt(w_rows, g_buf[...].reshape(HD, HD)).reshape(PLANE, 32, HD)[:, 0:20]

    for p in peers():
        send(o_send.at[p], r_o.at[pid], OUT, plane_dev(p))

    r_o[pid] = o_send[pid]
    wait_recv(r_o.at[pl.ds(0, PLANE - 1)], OUT)
    half[...] = jnp.sum(r_o[...], axis=0)
    last = pltpu.make_async_remote_copy(
        src_ref=half, dst_ref=r_half, send_sem=send_sem.at[CORE], recv_sem=recv_sem.at[CORE],
        device_id=(me, 1 - kv), device_id_type=MESH,
    )
    last.start()

    @pl.when(me == 0)
    def _():
        wait_send(units.at[pl.ds(0, 2 * heads - 1)], FIRST)

    @pl.when(near)
    def _():
        wait_send(part.at[pl.ds(0, PLANE - 1)], RS)

    @pl.when(jnp.logical_and(jnp.logical_not(near), owns_global))
    def _():
        wait_send(part.at[pl.ds(0, 7)], RS)

    @pl.when(jnp.logical_and(jnp.logical_not(near), owns_near))
    def _():
        wait_send(part.at[pl.ds(0, 8)], RS)

    wait_send(r_z.at[pl.ds(0, zs - 1)], ZRS)

    for slot in range(3):
        @pl.when(heads_me[slot])
        def _():
            wait_send(units.at[pl.ds(0, zs - 1)], PASS)

    @pl.when(owns_near)
    def _():
        wait_send(r_w.at[pl.ds(0, 7)], W)
        wait_send(r_w.at[pl.ds(0, 8), pl.ds(0, 3)], W)

    @pl.when(owns_global)
    def _():
        wait_send(r_w.at[pl.ds(0, 8)], W)
        wait_send(r_w.at[pl.ds(0, 7), pl.ds(0, 3)], W)

    wait_send(g_buf.at[pl.ds(0, zs - 1)], GATHER)
    wait_send(r_o.at[pl.ds(0, PLANE - 1)], OUT)
    last.wait()
    o_ref[...] = half[...] + r_half[...]


def solution(mesh):
    zs = mesh.shape["ctx"] // PLANE

    def local(*args):
        tokens, width = args[0].shape
        prompt, keys = args[4].shape
        cols = args[12].shape[0]
        heads = args[3].shape[1]
        any_spec = pl.BlockSpec(memory_space=pltpu.HBM)
        args = [jnp.transpose(a) if n in (3, 9) else a for n, a in enumerate(args)]
        out = pl.pallas_call(
            functools.partial(body, zs),
            out_shape=pltpu.VMEM((cols, prompt), F32),
            in_specs=[any_spec] * 18,
            out_specs=pl.BlockSpec(memory_space=pltpu.VMEM),
            scratch_shapes=[
                pltpu.VMEM((2, tokens, width), BF16),
                pltpu.VMEM((2, tokens, width), BF16),
                pltpu.VMEM((2, tokens, width), BF16),
                pltpu.VMEM((2, heads, tokens), F32),
                pltpu.VMEM((2, prompt, keys), BF16),
                pltpu.VMEM((2, prompt, keys), BF16),
                pltpu.VMEM((4, cols, PLANE * HD), BF16),
                pltpu.VMEM((PLANE, 4, cols, HD), BF16),
                pltpu.VMEM((PLANE, 32, 4 * HD), BF16),
                pltpu.VMEM((PLANE, HD, HD), BF16),
                pltpu.VMEM((PLANE, HD, HD), BF16),
                pltpu.VMEM((HD, HD), F32),
                pltpu.VMEM((zs, 8, HD), F32),
                pltpu.VMEM((zs, 8, HD), BF16),
                pltpu.VMEM((2 * heads, 80, HD), BF16),
                pltpu.VMEM((3, 80, HD), BF16),
                pltpu.VMEM((3, HD, HD), BF16),
                pltpu.VMEM((PLANE, cols, HD), F32),
                pltpu.VMEM((PLANE, cols, HD), F32),
                pltpu.VMEM((cols, HD), F32),
                pltpu.VMEM((cols, HD), F32),
                pltpu.SemaphoreType.DMA((20,)),
                pltpu.SemaphoreType.DMA((11,)),
                pltpu.SemaphoreType.DMA((11,)),
            ],
            compiler_params=pltpu.CompilerParams(
                collective_id=0, has_side_effects=True, vmem_limit_bytes=60 * 1024 * 1024
            ),
            name="prompt_grad",
        )(*args)
        return jnp.transpose(out)

    split = P("ctx", "kv")
    keys = P(None, "kv")
    layer = (split, split, split, split, keys, keys)
    return jax.shard_map(
        local,
        mesh=mesh,
        in_specs=layer + layer + (split,) * 6,
        out_specs=P(None, "ctx"),
        check_vma=False,
    )
```

```python
import functools

import jax
import jax.numpy as jnp
from jax import lax
from jax.experimental import pallas as pl
from jax.experimental.pallas import tpu as pltpu
from jax.sharding import PartitionSpec as P

HD = 128
HPG = 5
NEG = -1e30
PLANE = 16
MESH = pl.DeviceIdType.MESH
F32 = jnp.float32
BF16 = jnp.bfloat16


def nt(a, b):
    return lax.dot_general(a, b, (((1,), (1,)), ((), ())), preferred_element_type=F32)


def nn(a, b):
    return lax.dot_general(a, b, (((1,), (0,)), ((), ())), preferred_element_type=F32)


def unit_of(p):
    parity = (p % 4 + p // 4) % 2
    return p // 2 + 8 * (1 - parity)


OFFSETS = (
    (2, 2), (2, 1), (1, 2), (2, 3), (3, 2), (1, 1), (3, 3), (1, 3), (3, 1), (2, 0), (0, 2), (1, 0), (0, 1),
    (3, 0), (0, 3),
)


HEADS = ((0,) * 16, ((4,) * 4 + (12,) * 4) * 2, (12, 12, 0, 0, 4, 4, 0, 0))


def pos_of(u):
    return next(p for p in range(PLANE) if unit_of(p) == u)


def pack(ds):
    strips = [ds[16 * s:16 * (s + 1)] for s in range(8)]
    rows = [strips[0]]
    for s in range(1, 4):
        rows.append(strips[s] + pltpu.roll(strips[8 - s], 16 * s, 1))
    rows.append(strips[4])
    return jnp.concatenate(rows, axis=0)


def unpack(packed):
    lane = lax.broadcasted_iota(jnp.int32, (16, HD), 1)
    rows = [packed[16 * s:16 * (s + 1)] for s in range(5)]
    low = [jnp.where(lane >= 16 * s, rows[s], 0.0) for s in range(1, 4)]
    high = [
        jnp.where(lane >= HD - 16 * s, pltpu.roll(rows[s], HD - 16 * s, 1), 0.0) for s in range(3, 0, -1)
    ]
    return jnp.concatenate([rows[0]] + low + [rows[4]] + high, axis=0)


W, SLOT, RS, ZRS, PASS, GATHER, OUT, FIRST = 0, 1, 4, 5, 6, 7, 8, 9


def body(
    zs,
    sq, sdo, sout, slse, spk, spv,
    gq, gdo, gout, glse, gpk, gpv,
    wqs, wks, wvs, wqg, wkg, wvg,
    o_ref,
    q_buf, do_buf, out_buf, lse_buf, pk_buf, pv_buf,
    w_all, r_w, wp,
    part, r_kv, s_buf, r_z, g_buf,
    units, r_ds, key_t,
    o_acc, o_send, r_o,
    load_sem, send_sem, recv_sem, ready_sem,
):
    me = lax.axis_index("ctx")
    kv = lax.axis_index("kv")
    pid = lax.div(me, zs)
    z = lax.rem(me, zs)
    groups = pk_buf.shape[2] // HD
    heads = groups * HPG
    tokens = q_buf.shape[1]
    inv_root = HD ** (-0.5)
    near = pid < 4
    my_unit = unit_of(pid)
    owns_global = my_unit >= 8
    owns_near = my_unit < 8

    row, col = lax.div(pid, 4), lax.rem(pid, 4)

    def wrap(index, size):
        return jnp.where(index >= size, index - size, index)

    def peers():
        for dy, dx in OFFSETS:
            yield wrap(row + dy, 4) * 4 + wrap(col + dx, 4)

    def column():
        for k in range(zs - 1):
            half_way = zs // 2
            step = half_way + (k + 1) // 2 if k % 2 == 0 else half_way - (k + 1) // 2
            yield wrap(z + step, zs)

    def plane_dev(p):
        return (p * zs + z, kv)

    def z_dev(zz):
        return (pid * zs + zz, kv)

    def send(src, dst, phase, dev, arrive=None):
        pltpu.make_async_remote_copy(
            src_ref=src, dst_ref=dst, send_sem=send_sem.at[phase],
            recv_sem=recv_sem.at[phase if arrive is None else arrive],
            device_id=dev, device_id_type=MESH,
        ).start()

    def wait_recv(ref, phase):
        pltpu.make_async_copy(ref, ref, recv_sem.at[phase]).wait()

    def wait_send(ref, phase):
        pltpu.make_async_copy(ref, ref, send_sem.at[phase]).wait()

    heads_z = (
        0, jnp.where(my_unit // 4 % 2 == 0, 4, 12), jnp.where(my_unit % 4 < 2, jnp.where(my_unit < 4, 12, 4), 0),
    )
    heads_me = (
        z == 0, z == heads_z[1], jnp.logical_and(owns_near, z == heads_z[2]),
    )

    barrier = pltpu.get_barrier_semaphore()

    def greet(dev):
        pl.semaphore_signal(barrier, inc=1, device_id=dev, device_id_type=MESH)

    for zz in column():
        greet((pid * zs + zz, 1))

    for slot in (1, 2):
        @pl.when(jnp.logical_and(jnp.logical_and(pid != 0, z != 0), heads_me[slot]))
        def _():
            greet((0, 1))

    def tell(sem):
        pl.semaphore_signal(sem, inc=1, device_id=(me, 1 - kv), device_id_type=MESH)

    def plane_ready():
        @pl.when(kv == 0)
        def _():
            pl.semaphore_wait(barrier, 2 * (PLANE - 1) + 1)
            tell(ready_sem.at[0])

        @pl.when(kv == 1)
        def _():
            pl.semaphore_wait(ready_sem.at[0], 1)

    def z_ready():
        @pl.when(kv == 1)
        def _():
            greeted = 2 * (zs - 1) + 1
            pl.semaphore_wait(barrier, jnp.where(me == 0, greeted + 38, greeted))
            tell(ready_sem.at[1])

        @pl.when(kv == 0)
        def _():
            pl.semaphore_wait(ready_sem.at[1], 1)

    keys = groups * HD
    cut = 2048 - heads * HD
    layer_loads = []
    for layer, srcs in enumerate(((sq, sdo, sout, slse, spv, spk), (gq, gdo, gout, glse, gpv, gpk))):
        dsts = (q_buf, do_buf, out_buf, lse_buf, pv_buf, pk_buf)
        layer_loads.append([
            pltpu.make_async_copy(s, d.at[layer], load_sem.at[8 + 6 * layer + n])
            for n, (s, d) in enumerate(zip(srcs, dsts))
        ])
    w_srcs = (
        (wks, 0, 0, 0, keys), (wvs, 0, 0, keys, keys), (wkg, 0, 0, 2 * keys, keys), (wvg, 0, 0, 3 * keys, keys),
        (wqg, 0, 1, 0, 2048), (wqg, 2048, 2, 0, 512), (wqs, 0, 2, 512, 1536), (wqs, 1536, 3, 0, 1024),
    )
    w_loads = [
        pltpu.make_async_copy(
            src.at[:, pl.ds(first, size)], w_all.at[slot, :, pl.ds(start, size)], load_sem.at[n]
        )
        for n, (src, first, slot, start, size) in enumerate(w_srcs)
    ]
    for c in layer_loads[1]:
        c.start()

    for p in peers():
        greet((p * zs + z, 0))

    greet((me, 1 - kv))
    layer_loads[0][5].start()

    @pl.when(near)
    def _():
        for c in layer_loads[0][:5]:
            c.start()

    for c in w_loads:
        c.start()

    wp[...] = jnp.zeros_like(wp)

    rows = lax.broadcasted_iota(jnp.int32, (HD, tokens), 0)
    cols = lax.broadcasted_iota(jnp.int32, (HD, tokens), 1) + me * tokens
    allowed = rows <= cols
    ones = jnp.ones((16, 2 * HD), BF16)

    def group_terms(layer, g):
        spans = [pl.ds((g * HPG + h) * HD, HD) for h in range(HPG)]
        q_cat = jnp.concatenate([q_buf[layer, :, s] for s in spans], axis=0)
        do_cat = jnp.concatenate([do_buf[layer, :, s] for s in spans], axis=0)
        out_cat = jnp.concatenate([out_buf[layer, :, s] for s in spans], axis=0)
        key = pk_buf[layer, :, g * HD:(g + 1) * HD]
        val = pv_buf[layer, :, g * HD:(g + 1) * HD]
        prod = do_cat.astype(F32) * out_cat.astype(F32)
        high = prod.astype(BF16)
        low = (prod - high.astype(F32)).astype(BF16)
        delta = nt(ones, jnp.concatenate([high, low], axis=1))
        scores = nt(key, q_cat)
        grad_prob = nt(val, do_cat)
        p_parts, ds_parts = [], []
        for h in range(HPG):
            span = slice(h * tokens, (h + 1) * tokens)
            row = g * HPG + h
            arg = scores[:, span] * inv_root - lse_buf[layer, row:row + 1, :]
            probs = jnp.exp(jnp.where(allowed, arg, NEG))
            p_parts.append(probs.astype(BF16))
            ds_parts.append((probs * (grad_prob[:, span] - delta[0:1, span])).astype(BF16))
        part[8 * layer + g] = (nn(jnp.concatenate(ds_parts, axis=1), q_cat) * inv_root).astype(BF16)
        part[8 * layer + 4 + g] = nn(jnp.concatenate(p_parts, axis=1), do_cat).astype(BF16)

        @pl.when(me == 0)
        def _():
            for h in range(HPG):
                units[(1 - layer) * heads + g * HPG + h] = pack(ds_parts[h].astype(F32)).astype(BF16)

    def send_units(slots):
        for dy, dx in OFFSETS + ((0, 0),):
            p = 4 * dy + dx
            u = unit_of(p)
            for slot in (t for t in slots if t < 2 or u < 8):
                n = 16 * slot + u
                head = HEADS[slot][u]
                if p == 0 and head == 0:
                    r_ds[slot] = units[n]
                else:
                    send(units.at[n], r_ds.at[slot], FIRST, (p * zs + head, kv), SLOT + slot)

    for c in layer_loads[1]:
        c.wait()
    for g in range(groups):
        group_terms(1, g)
    plane_ready()

    for p in peers():
        u = unit_of(p)

        @pl.when(u >= 8)
        def _():
            send(part.at[u], r_kv.at[pid], RS, plane_dev(p))

    layer_loads[0][5].wait()

    @pl.when(near)
    def _():
        for c in layer_loads[0][:5]:
            c.wait()
        for g in range(groups):
            group_terms(0, g)
            for u in (g, 4 + g):
                p = pos_of(u)

                @pl.when(pid != p)
                def _():
                    send(part.at[u], r_kv.at[pid], RS, plane_dev(p))

    @pl.when(me == 0)
    def _():
        send_units((0,))

    z_ready()

    @pl.when(me == 0)
    def _():
        send_units((1, 2))

    @pl.when(jnp.logical_or(near, owns_global))
    def _():
        r_kv[pid] = part[my_unit]

    for c in w_loads:
        c.wait()

    @pl.when(owns_global)
    def _():
        wait_recv(r_kv.at[pl.ds(0, PLANE - 1)], RS)
        acc = r_kv[0].astype(F32)
        for n in range(1, PLANE):
            acc = acc + r_kv[n].astype(F32)
        s_buf[...] = acc

    @pl.when(owns_near)
    def _():
        @pl.when(near)
        def _():
            wait_recv(r_kv.at[pl.ds(0, 3)], RS)

        @pl.when(jnp.logical_not(near))
        def _():
            wait_recv(r_kv.at[pl.ds(0, 4)], RS)

        acc = r_kv[0].astype(F32)
        for n in range(1, 4):
            acc = acc + r_kv[n].astype(F32)
        s_buf[...] = acc

    for zz in column():
        send(s_buf.at[pl.ds(pl.multiple_of(8 * zz, 8), 8)], r_z.at[z], ZRS, z_dev(zz))

    r_z[z] = s_buf[pl.ds(pl.multiple_of(8 * z, 8), 8), :]

    def pass_on(slot):
        @pl.when(pid != 0 if slot == 0 else me >= 0)
        def _():
            wait_recv(r_ds.at[slot], SLOT + slot)

        for zz in column():
            send(r_ds.at[slot], r_ds.at[slot], PASS, z_dev(zz), SLOT + slot)

    for p in peers():
        u = unit_of(p)
        lanes = pl.ds(pl.multiple_of(u * HD, HD), HD)

        @pl.when(u < 8)
        def _():
            send(w_all.at[:, :, lanes], r_w.at[pid], W, plane_dev(p))

        @pl.when(u >= 8)
        def _():
            send(w_all.at[pl.ds(0, 3), :, lanes], r_w.at[pid, pl.ds(0, 3)], W, plane_dev(p))

    @pl.when(heads_me[0])
    def _():
        pass_on(0)

    def make_key(slot):
        n = 16 * slot + my_unit
        layer = jnp.where(n < heads, 1, 0)
        g = (n % heads) // HPG
        key = pk_buf[layer, :, pl.ds(pl.multiple_of(g * HD, HD), HD)]
        key_t[slot] = jnp.transpose(key.astype(F32)).astype(BF16)

    my_lanes = pl.ds(pl.multiple_of(my_unit * HD, HD), HD)
    for slot in range(3):
        r_w[pid, slot] = w_all[slot, :, my_lanes]
    make_key(0)
    make_key(1)

    @pl.when(owns_near)
    def _():
        r_w[pid, 3] = w_all[3, :, my_lanes]
        make_key(2)

    wait_recv(r_z.at[pl.ds(0, zs - 1)], ZRS)
    g_buf[z] = jnp.sum(r_z[...], axis=0).astype(BF16)

    for zz in column():
        send(g_buf.at[z], g_buf.at[z], GATHER, z_dev(zz))

    @pl.when(heads_me[1])
    def _():
        pass_on(1)

    @pl.when(heads_me[2])
    def _():
        pass_on(2)

    @pl.when(owns_near)
    def _():
        wait_recv(r_w.at[pl.ds(0, PLANE - 1)], W)
        wp[:, 0:20, 384:512] = r_w[:, 3]

    @pl.when(owns_global)
    def _():
        wait_recv(r_w.at[pl.ds(0, PLANE - 1), pl.ds(0, 3)], W)

    for slot in range(3):
        wp[:, 0:20, slot * HD:(slot + 1) * HD] = r_w[:, slot]

    def project(slot):
        ds = unpack(r_ds[slot].astype(F32)).astype(BF16)
        grad_q = (nn(key_t[slot], ds) * inv_root).astype(BF16)
        w_rows = wp[:, :, (slot + 1) * HD:(slot + 2) * HD].reshape(PLANE * 32, HD)
        return nn(w_rows, grad_q).reshape(PLANE, 32, HD)[:, 0:20]

    for slot in range(2):
        @pl.when(z != heads_z[slot])
        def _():
            wait_recv(r_ds.at[slot], SLOT + slot)

    o_acc[...] = project(0) + project(1)

    @pl.when(owns_near)
    def _():
        @pl.when(z != heads_z[2])
        def _():
            wait_recv(r_ds.at[2], SLOT + 2)

        o_acc[...] += project(2)

    wait_recv(g_buf.at[pl.ds(0, zs - 1)], GATHER)
    w_rows = wp[:, :, 0:HD].reshape(PLANE * 32, HD)
    last_term = nt(w_rows, g_buf[...].reshape(HD, HD)).reshape(PLANE, 32, HD)[:, 0:20]
    o_send[...] = (o_acc[...] + last_term).astype(o_send.dtype)

    mine = PLANE * kv + pid
    for p in peers():
        for core in range(2):
            send(o_send.at[p], r_o.at[mine], OUT, (p * zs + z, core))
    send(o_send.at[pid], r_o.at[mine], OUT, (me, 1 - kv))
    r_o[mine] = o_send[pid]

    @pl.when(me == 0)
    def _():
        wait_send(units.at[pl.ds(0, 2 * heads - 1)], FIRST)

    @pl.when(near)
    def _():
        wait_send(part.at[pl.ds(0, PLANE - 1)], RS)

    @pl.when(jnp.logical_and(jnp.logical_not(near), owns_global))
    def _():
        wait_send(part.at[pl.ds(0, 7)], RS)

    @pl.when(jnp.logical_and(jnp.logical_not(near), owns_near))
    def _():
        wait_send(part.at[pl.ds(0, 8)], RS)

    wait_send(r_z.at[pl.ds(0, zs - 1)], ZRS)

    for slot in range(3):
        @pl.when(heads_me[slot])
        def _():
            wait_send(units.at[pl.ds(0, zs - 1)], PASS)

    @pl.when(owns_near)
    def _():
        wait_send(r_w.at[pl.ds(0, 7)], W)
        wait_send(r_w.at[pl.ds(0, 8), pl.ds(0, 3)], W)

    @pl.when(owns_global)
    def _():
        wait_send(r_w.at[pl.ds(0, 8)], W)
        wait_send(r_w.at[pl.ds(0, 7), pl.ds(0, 3)], W)

    wait_send(g_buf.at[pl.ds(0, zs - 1)], GATHER)
    wait_send(r_o.at[pl.ds(0, 2 * PLANE - 1)], OUT)
    wait_recv(r_o.at[pl.ds(0, 2 * PLANE - 1)], OUT)
    o_ref[...] = jnp.sum(r_o[...].astype(F32), axis=0)


def solution(mesh):
    zs = mesh.shape["ctx"] // PLANE

    def local(*args):
        tokens, width = args[0].shape
        prompt, keys = args[4].shape
        cols = args[12].shape[0]
        heads = args[3].shape[1]
        any_spec = pl.BlockSpec(memory_space=pltpu.HBM)
        args = [jnp.transpose(a) if n in (3, 9) else a for n, a in enumerate(args)]
        out = pl.pallas_call(
            functools.partial(body, zs),
            out_shape=pltpu.VMEM((cols, prompt), F32),
            in_specs=[any_spec] * 18,
            out_specs=pl.BlockSpec(memory_space=pltpu.VMEM),
            scratch_shapes=[
                pltpu.VMEM((2, tokens, width), BF16),
                pltpu.VMEM((2, tokens, width), BF16),
                pltpu.VMEM((2, tokens, width), BF16),
                pltpu.VMEM((2, heads, tokens), F32),
                pltpu.VMEM((2, prompt, keys), BF16),
                pltpu.VMEM((2, prompt, keys), BF16),
                pltpu.VMEM((4, cols, PLANE * HD), BF16),
                pltpu.VMEM((PLANE, 4, cols, HD), BF16),
                pltpu.VMEM((PLANE, 32, 4 * HD), BF16),
                pltpu.VMEM((PLANE, HD, HD), BF16),
                pltpu.VMEM((PLANE, HD, HD), BF16),
                pltpu.VMEM((HD, HD), F32),
                pltpu.VMEM((zs, 8, HD), F32),
                pltpu.VMEM((zs, 8, HD), BF16),
                pltpu.VMEM((2 * heads, 80, HD), BF16),
                pltpu.VMEM((3, 80, HD), BF16),
                pltpu.VMEM((3, HD, HD), BF16),
                pltpu.VMEM((PLANE, cols, HD), F32),
                pltpu.VMEM((PLANE, cols, HD), F32),
                pltpu.VMEM((2 * PLANE, cols, HD), F32),
                pltpu.SemaphoreType.DMA((20,)),
                pltpu.SemaphoreType.DMA((10,)),
                pltpu.SemaphoreType.DMA((10,)),
                pltpu.SemaphoreType.REGULAR((2,)),
            ],
            compiler_params=pltpu.CompilerParams(
                collective_id=0, has_side_effects=True, vmem_limit_bytes=60 * 1024 * 1024
            ),
            name="prompt_grad",
        )(*args)
        return jnp.transpose(out)

    split = P("ctx", "kv")
    keys = P(None, "kv")
    layer = (split, split, split, split, keys, keys)
    return jax.shard_map(
        local,
        mesh=mesh,
        in_specs=layer + layer + (split,) * 6,
        out_specs=P(None, "ctx"),
        check_vma=False,
    )
```

```python
import functools

import jax
import jax.numpy as jnp
from jax import lax
from jax.experimental import pallas as pl
from jax.experimental.pallas import tpu as pltpu
from jax.sharding import PartitionSpec as P

HD = 128
HPG = 5
NEG = -1e30
PLANE = 16
MESH = pl.DeviceIdType.MESH
F32 = jnp.float32
BF16 = jnp.bfloat16


def nt(a, b):
    return lax.dot_general(a, b, (((1,), (1,)), ((), ())), preferred_element_type=F32)


def nn(a, b):
    return lax.dot_general(a, b, (((1,), (0,)), ((), ())), preferred_element_type=F32)


def unit_of(p):
    parity = (p % 4 + p // 4) % 2
    return p // 2 + 8 * (1 - parity)


OFFSETS = (
    (2, 2), (2, 1), (1, 2), (2, 3), (3, 2), (1, 1), (3, 3), (1, 3), (3, 1), (2, 0), (0, 2), (1, 0), (0, 1),
    (3, 0), (0, 3),
)


HEADS = ((0,) * 16, ((4,) * 4 + (12,) * 4) * 2, (12, 12, 0, 0, 4, 4, 0, 0))


def pos_of(u):
    return next(p for p in range(PLANE) if unit_of(p) == u)


STRIP = 8
HALF = HD // STRIP // 2
PACKED = STRIP * (HALF + 1)


def pack(ds):
    strips = [ds[STRIP * s:STRIP * (s + 1)] for s in range(2 * HALF)]
    rows = [strips[0]]
    for s in range(1, HALF):
        rows.append(strips[s] + pltpu.roll(strips[2 * HALF - s], STRIP * s, 1))
    rows.append(strips[HALF])
    return jnp.concatenate(rows, axis=0)


def unpack(packed):
    lane = lax.broadcasted_iota(jnp.int32, (STRIP, HD), 1)
    rows = [packed[STRIP * s:STRIP * (s + 1)] for s in range(HALF + 1)]
    low = [jnp.where(lane >= STRIP * s, rows[s], 0.0) for s in range(1, HALF)]
    high = [
        jnp.where(lane >= HD - STRIP * s, pltpu.roll(rows[s], HD - STRIP * s, 1), 0.0)
        for s in range(HALF - 1, 0, -1)
    ]
    return jnp.concatenate([rows[0]] + low + [rows[HALF]] + high, axis=0)


W, SLOT, RS, ZRS, PASS, GATHER, OUT, FIRST = 0, 1, 4, 5, 6, 7, 8, 9


def body(
    zs,
    sq, sdo, sout, slse, spk, spv,
    gq, gdo, gout, glse, gpk, gpv,
    wqs, wks, wvs, wqg, wkg, wvg,
    o_ref,
    q_buf, do_buf, out_buf, lse_buf, pk_buf, pv_buf,
    w_all, r_w, wp,
    part, r_kv, s_buf, r_z, g_buf,
    units, r_ds, key_t,
    o_acc, o_send, r_o,
    load_sem, send_sem, recv_sem, ready_sem,
):
    me = lax.axis_index("ctx")
    kv = lax.axis_index("kv")
    pid = lax.div(me, zs)
    z = lax.rem(me, zs)
    groups = pk_buf.shape[2] // HD
    heads = groups * HPG
    tokens = q_buf.shape[1]
    inv_root = HD ** (-0.5)
    near = pid < 4
    my_unit = unit_of(pid)
    owns_global = my_unit >= 8
    owns_near = my_unit < 8

    row, col = lax.div(pid, 4), lax.rem(pid, 4)

    def wrap(index, size):
        return jnp.where(index >= size, index - size, index)

    def peers():
        for dy, dx in OFFSETS:
            yield wrap(row + dy, 4) * 4 + wrap(col + dx, 4)

    def column():
        for k in range(zs - 1):
            half_way = zs // 2
            step = half_way + (k + 1) // 2 if k % 2 == 0 else half_way - (k + 1) // 2
            yield wrap(z + step, zs)

    def plane_dev(p):
        return (p * zs + z, kv)

    def z_dev(zz):
        return (pid * zs + zz, kv)

    def send(src, dst, phase, dev, arrive=None):
        pltpu.make_async_remote_copy(
            src_ref=src, dst_ref=dst, send_sem=send_sem.at[phase],
            recv_sem=recv_sem.at[phase if arrive is None else arrive],
            device_id=dev, device_id_type=MESH,
        ).start()

    def wait_recv(ref, phase):
        pltpu.make_async_copy(ref, ref, recv_sem.at[phase]).wait()

    def wait_send(ref, phase):
        pltpu.make_async_copy(ref, ref, send_sem.at[phase]).wait()

    heads_z = (
        0, jnp.where(my_unit // 4 % 2 == 0, 4, 12), jnp.where(my_unit % 4 < 2, jnp.where(my_unit < 4, 12, 4), 0),
    )
    heads_me = (
        z == 0, z == heads_z[1], jnp.logical_and(owns_near, z == heads_z[2]),
    )

    barrier = pltpu.get_barrier_semaphore()

    def greet(dev):
        pl.semaphore_signal(barrier, inc=1, device_id=dev, device_id_type=MESH)

    for zz in column():
        greet((pid * zs + zz, 1))

    for slot in (1, 2):
        @pl.when(jnp.logical_and(jnp.logical_and(pid != 0, z != 0), heads_me[slot]))
        def _():
            greet((0, 1))

    def tell(sem):
        pl.semaphore_signal(sem, inc=1, device_id=(me, 1 - kv), device_id_type=MESH)

    def plane_ready():
        @pl.when(kv == 0)
        def _():
            pl.semaphore_wait(barrier, 2 * (PLANE - 1) + 1)
            tell(ready_sem.at[0])

        @pl.when(kv == 1)
        def _():
            pl.semaphore_wait(ready_sem.at[0], 1)

    def z_ready():
        @pl.when(kv == 1)
        def _():
            greeted = 2 * (zs - 1) + 1
            pl.semaphore_wait(barrier, jnp.where(me == 0, greeted + 38, greeted))
            tell(ready_sem.at[1])

        @pl.when(kv == 0)
        def _():
            pl.semaphore_wait(ready_sem.at[1], 1)

    keys = groups * HD
    cut = 2048 - heads * HD
    layer_loads = []
    for layer, srcs in enumerate(((sq, sdo, sout, slse, spv, spk), (gq, gdo, gout, glse, gpv, gpk))):
        dsts = (q_buf, do_buf, out_buf, lse_buf, pv_buf, pk_buf)
        layer_loads.append([
            pltpu.make_async_copy(s, d.at[layer], load_sem.at[8 + 6 * layer + n])
            for n, (s, d) in enumerate(zip(srcs, dsts))
        ])
    w_srcs = (
        (wks, 0, 0, 0, keys), (wvs, 0, 0, keys, keys), (wkg, 0, 0, 2 * keys, keys), (wvg, 0, 0, 3 * keys, keys),
        (wqg, 0, 1, 0, 2048), (wqg, 2048, 2, 0, 512), (wqs, 0, 2, 512, 1536), (wqs, 1536, 3, 0, 1024),
    )
    w_loads = [
        pltpu.make_async_copy(
            src.at[:, pl.ds(first, size)], w_all.at[slot, :, pl.ds(start, size)], load_sem.at[n]
        )
        for n, (src, first, slot, start, size) in enumerate(w_srcs)
    ]
    for c in layer_loads[1]:
        c.start()

    for p in peers():
        greet((p * zs + z, 0))

    greet((me, 1 - kv))
    layer_loads[0][5].start()

    @pl.when(near)
    def _():
        for c in layer_loads[0][:5]:
            c.start()

    for c in w_loads:
        c.start()

    wp[...] = jnp.zeros_like(wp)

    rows = lax.broadcasted_iota(jnp.int32, (HD, tokens), 0)
    cols = lax.broadcasted_iota(jnp.int32, (HD, tokens), 1) + me * tokens
    allowed = rows <= cols
    ones = jnp.ones((16, 2 * HD), BF16)

    def group_terms(layer, g):
        spans = [pl.ds((g * HPG + h) * HD, HD) for h in range(HPG)]
        q_cat = jnp.concatenate([q_buf[layer, :, s] for s in spans], axis=0)
        do_cat = jnp.concatenate([do_buf[layer, :, s] for s in spans], axis=0)
        out_cat = jnp.concatenate([out_buf[layer, :, s] for s in spans], axis=0)
        key = pk_buf[layer, :, g * HD:(g + 1) * HD]
        val = pv_buf[layer, :, g * HD:(g + 1) * HD]
        prod = do_cat.astype(F32) * out_cat.astype(F32)
        high = prod.astype(BF16)
        low = (prod - high.astype(F32)).astype(BF16)
        delta = nt(ones, jnp.concatenate([high, low], axis=1))
        scores = nt(key, q_cat)
        grad_prob = nt(val, do_cat)
        p_parts, ds_parts = [], []
        for h in range(HPG):
            span = slice(h * tokens, (h + 1) * tokens)
            row = g * HPG + h
            arg = scores[:, span] * inv_root - lse_buf[layer, row:row + 1, :]
            probs = jnp.exp(jnp.where(allowed, arg, NEG))
            p_parts.append(probs.astype(BF16))
            ds_parts.append((probs * (grad_prob[:, span] - delta[0:1, span])).astype(BF16))
        part[8 * layer + g] = (nn(jnp.concatenate(ds_parts, axis=1), q_cat) * inv_root).astype(BF16)
        part[8 * layer + 4 + g] = nn(jnp.concatenate(p_parts, axis=1), do_cat).astype(BF16)

        @pl.when(me == 0)
        def _():
            for h in range(HPG):
                units[(1 - layer) * heads + g * HPG + h] = pack(ds_parts[h].astype(F32)).astype(BF16)

    def send_units(slots):
        for dy, dx in OFFSETS + ((0, 0),):
            p = 4 * dy + dx
            u = unit_of(p)
            for slot in (t for t in slots if t < 2 or u < 8):
                n = 16 * slot + u
                head = HEADS[slot][u]
                if p == 0 and head == 0:
                    r_ds[slot] = units[n]
                else:
                    send(units.at[n], r_ds.at[slot], FIRST, (p * zs + head, kv), SLOT + slot)

    for c in layer_loads[1]:
        c.wait()
    for g in range(groups):
        group_terms(1, g)
    plane_ready()

    for p in peers():
        u = unit_of(p)

        @pl.when(u >= 8)
        def _():
            send(part.at[u], r_kv.at[pid], RS, plane_dev(p))

    @pl.when(me == 0)
    def _():
        send_units((0,))

    layer_loads[0][5].wait()

    @pl.when(near)
    def _():
        for c in layer_loads[0][:5]:
            c.wait()
        for g in range(groups):
            group_terms(0, g)
            for u in (g, 4 + g):
                p = pos_of(u)

                @pl.when(pid != p)
                def _():
                    send(part.at[u], r_kv.at[pid], RS, plane_dev(p))

    z_ready()

    @pl.when(me == 0)
    def _():
        send_units((1, 2))

    @pl.when(jnp.logical_or(near, owns_global))
    def _():
        r_kv[pid] = part[my_unit]

    for c in w_loads:
        c.wait()

    @pl.when(owns_global)
    def _():
        wait_recv(r_kv.at[pl.ds(0, PLANE - 1)], RS)
        acc = r_kv[0].astype(F32)
        for n in range(1, PLANE):
            acc = acc + r_kv[n].astype(F32)
        s_buf[...] = acc

    @pl.when(owns_near)
    def _():
        @pl.when(near)
        def _():
            wait_recv(r_kv.at[pl.ds(0, 3)], RS)

        @pl.when(jnp.logical_not(near))
        def _():
            wait_recv(r_kv.at[pl.ds(0, 4)], RS)

        acc = r_kv[0].astype(F32)
        for n in range(1, 4):
            acc = acc + r_kv[n].astype(F32)
        s_buf[...] = acc

    for zz in column():
        send(s_buf.at[pl.ds(pl.multiple_of(8 * zz, 8), 8)], r_z.at[z], ZRS, z_dev(zz))

    r_z[z] = s_buf[pl.ds(pl.multiple_of(8 * z, 8), 8), :]

    def pass_on(slot):
        @pl.when(pid != 0 if slot == 0 else me >= 0)
        def _():
            wait_recv(r_ds.at[slot], SLOT + slot)

        for zz in column():
            send(r_ds.at[slot], r_ds.at[slot], PASS, z_dev(zz), SLOT + slot)

    @pl.when(heads_me[0])
    def _():
        pass_on(0)

    for p in peers():
        u = unit_of(p)
        lanes = pl.ds(pl.multiple_of(u * HD, HD), HD)

        @pl.when(u < 8)
        def _():
            send(w_all.at[:, :, lanes], r_w.at[pid], W, plane_dev(p))

        @pl.when(u >= 8)
        def _():
            send(w_all.at[pl.ds(0, 3), :, lanes], r_w.at[pid, pl.ds(0, 3)], W, plane_dev(p))

    def make_key(slot):
        n = 16 * slot + my_unit
        layer = jnp.where(n < heads, 1, 0)
        g = (n % heads) // HPG
        key = pk_buf[layer, :, pl.ds(pl.multiple_of(g * HD, HD), HD)]
        key_t[slot] = jnp.transpose(key.astype(F32)).astype(BF16)

    my_lanes = pl.ds(pl.multiple_of(my_unit * HD, HD), HD)
    for slot in range(3):
        r_w[pid, slot] = w_all[slot, :, my_lanes]
    make_key(0)
    make_key(1)

    @pl.when(owns_near)
    def _():
        r_w[pid, 3] = w_all[3, :, my_lanes]
        make_key(2)

    wait_recv(r_z.at[pl.ds(0, zs - 1)], ZRS)
    g_buf[z] = jnp.sum(r_z[...], axis=0).astype(BF16)

    for zz in column():
        send(g_buf.at[z], g_buf.at[z], GATHER, z_dev(zz))

    @pl.when(heads_me[1])
    def _():
        pass_on(1)

    @pl.when(heads_me[2])
    def _():
        pass_on(2)

    @pl.when(owns_near)
    def _():
        wait_recv(r_w.at[pl.ds(0, PLANE - 1)], W)
        wp[:, 0:20, 384:512] = r_w[:, 3]

    @pl.when(owns_global)
    def _():
        wait_recv(r_w.at[pl.ds(0, PLANE - 1), pl.ds(0, 3)], W)

    for slot in range(3):
        wp[:, 0:20, slot * HD:(slot + 1) * HD] = r_w[:, slot]

    def project(slot):
        ds = unpack(r_ds[slot].astype(F32)).astype(BF16)
        grad_q = (nn(key_t[slot], ds) * inv_root).astype(BF16)
        w_rows = wp[:, :, (slot + 1) * HD:(slot + 2) * HD].reshape(PLANE * 32, HD)
        return nn(w_rows, grad_q).reshape(PLANE, 32, HD)[:, 0:20]

    for slot in range(2):
        @pl.when(z != heads_z[slot])
        def _():
            wait_recv(r_ds.at[slot], SLOT + slot)

    o_acc[...] = project(0) + project(1)

    @pl.when(owns_near)
    def _():
        @pl.when(z != heads_z[2])
        def _():
            wait_recv(r_ds.at[2], SLOT + 2)

        o_acc[...] += project(2)

    wait_recv(g_buf.at[pl.ds(0, zs - 1)], GATHER)
    w_rows = wp[:, :, 0:HD].reshape(PLANE * 32, HD)
    last_term = nt(w_rows, g_buf[...].reshape(HD, HD)).reshape(PLANE, 32, HD)[:, 0:20]
    o_send[...] = (o_acc[...] + last_term).astype(o_send.dtype)

    mine = PLANE * kv + pid
    for p in peers():
        for core in range(2):
            send(o_send.at[p], r_o.at[mine], OUT, (p * zs + z, core))
    send(o_send.at[pid], r_o.at[mine], OUT, (me, 1 - kv))
    r_o[mine] = o_send[pid]

    @pl.when(me == 0)
    def _():
        wait_send(units.at[pl.ds(0, 2 * heads - 1)], FIRST)

    @pl.when(near)
    def _():
        wait_send(part.at[pl.ds(0, PLANE - 1)], RS)

    @pl.when(jnp.logical_and(jnp.logical_not(near), owns_global))
    def _():
        wait_send(part.at[pl.ds(0, 7)], RS)

    @pl.when(jnp.logical_and(jnp.logical_not(near), owns_near))
    def _():
        wait_send(part.at[pl.ds(0, 8)], RS)

    wait_send(r_z.at[pl.ds(0, zs - 1)], ZRS)

    for slot in range(3):
        @pl.when(heads_me[slot])
        def _():
            wait_send(units.at[pl.ds(0, zs - 1)], PASS)

    @pl.when(owns_near)
    def _():
        wait_send(r_w.at[pl.ds(0, 7)], W)
        wait_send(r_w.at[pl.ds(0, 8), pl.ds(0, 3)], W)

    @pl.when(owns_global)
    def _():
        wait_send(r_w.at[pl.ds(0, 8)], W)
        wait_send(r_w.at[pl.ds(0, 7), pl.ds(0, 3)], W)

    wait_send(g_buf.at[pl.ds(0, zs - 1)], GATHER)
    wait_send(r_o.at[pl.ds(0, 2 * PLANE - 1)], OUT)
    wait_recv(r_o.at[pl.ds(0, 2 * PLANE - 1)], OUT)
    o_ref[...] = jnp.sum(r_o[...].astype(F32), axis=0)


def solution(mesh):
    zs = mesh.shape["ctx"] // PLANE

    def local(*args):
        tokens, width = args[0].shape
        prompt, keys = args[4].shape
        cols = args[12].shape[0]
        heads = args[3].shape[1]
        any_spec = pl.BlockSpec(memory_space=pltpu.HBM)
        args = [jnp.transpose(a) if n in (3, 9) else a for n, a in enumerate(args)]
        out = pl.pallas_call(
            functools.partial(body, zs),
            out_shape=pltpu.VMEM((cols, prompt), F32),
            in_specs=[any_spec] * 18,
            out_specs=pl.BlockSpec(memory_space=pltpu.VMEM),
            scratch_shapes=[
                pltpu.VMEM((2, tokens, width), BF16),
                pltpu.VMEM((2, tokens, width), BF16),
                pltpu.VMEM((2, tokens, width), BF16),
                pltpu.VMEM((2, heads, tokens), F32),
                pltpu.VMEM((2, prompt, keys), BF16),
                pltpu.VMEM((2, prompt, keys), BF16),
                pltpu.VMEM((4, cols, PLANE * HD), BF16),
                pltpu.VMEM((PLANE, 4, cols, HD), BF16),
                pltpu.VMEM((PLANE, 32, 4 * HD), BF16),
                pltpu.VMEM((PLANE, HD, HD), BF16),
                pltpu.VMEM((PLANE, HD, HD), BF16),
                pltpu.VMEM((HD, HD), F32),
                pltpu.VMEM((zs, 8, HD), F32),
                pltpu.VMEM((zs, 8, HD), BF16),
                pltpu.VMEM((2 * heads, PACKED, HD), BF16),
                pltpu.VMEM((3, PACKED, HD), BF16),
                pltpu.VMEM((3, HD, HD), BF16),
                pltpu.VMEM((PLANE, cols, HD), F32),
                pltpu.VMEM((PLANE, cols, HD), F32),
                pltpu.VMEM((2 * PLANE, cols, HD), F32),
                pltpu.SemaphoreType.DMA((20,)),
                pltpu.SemaphoreType.DMA((10,)),
                pltpu.SemaphoreType.DMA((10,)),
                pltpu.SemaphoreType.REGULAR((2,)),
            ],
            compiler_params=pltpu.CompilerParams(
                collective_id=0, has_side_effects=True, vmem_limit_bytes=60 * 1024 * 1024
            ),
            name="prompt_grad",
        )(*args)
        return jnp.transpose(out)

    split = P("ctx", "kv")
    keys = P(None, "kv")
    layer = (split, split, split, split, keys, keys)
    return jax.shard_map(
        local,
        mesh=mesh,
        in_specs=layer + layer + (split,) * 6,
        out_specs=P(None, "ctx"),
        check_vma=False,
    )
```
